256 devices in a mesh: row: 16 (over x, z_hi), col: 16 (over y, z_lo, core).
Axes of the slice: x: 4, y: 4, z: 8 (z_hi: 4, z_lo: 2; z = z_hi * 2 + z_lo), core: 2. Of those that a mesh axis runs over, the one named last changes fastest.
Arguments:
- tile_count: int32 [16, 16], P('row', 'col'), may hold values from 1 to 40, as said below
- tile_rows: int32 [16, 16, 40], P('row', 'col'), may hold values from 0 to 31, as said below
- tile_cols: int32 [16, 16, 40], P('row', 'col'), may hold values from 0 to 31, as said below
- tiles: float32 [16, 16, 40, 256, 256], P('row', 'col')
- block: float32 [64, 131072], P(None, ('row', 'col')), may hold values from -6 to 6
Outputs:
- image_x: float32 [64, 131072], P(None, ('row', 'col'))
- image_w: float32 [64, 131072], P(None, ('row', 'col'))
- grams: float32 [4, 64, 64], replicated
The draws below stay inside these ranges and needn't reach their ends.
Inputs may be any that keep to these rules, and one draw needn't show every extreme that they name: `tile_count`: live slots of each grid block; the largest count over the grid is exactly 40. `tile_rows`: live slots of one grid block hold distinct positions whose global tile row is at least the global tile column; slots at or past the count hold 0. `tile_cols`: paired with tile_rows as above; slots at or past the count hold 0.
All inputs are finite; a program needn't handle non-finite values.
Results may differ from the reference program's by a relative error of at most 0.0001.
Values sent between devices are 32-bit elements; how exact they have to be, the bound alone decides.
A program may use at most 64 MiB of HBM per device.

```python
import jax
import jax.numpy as jnp
from jax import lax

K = 64
TILE = 256
SEG_T = 2
TILES_DEV = 40
N = 131072
N_ROW = 16
N_COL = 16


def tile_layout(key):
    base = jax.random.fold_in(key, 7)
    key_jitter = jax.random.fold_in(base, 1)
    key_order = jax.random.fold_in(base, 2)
    row_span = N_COL * SEG_T
    col_span = N_ROW * SEG_T
    places = row_span * col_span
    row_pos = jnp.arange(N_ROW, dtype=jnp.int32)[:, None, None]
    col_pos = jnp.arange(N_COL, dtype=jnp.int32)[None, :, None]
    flat = jnp.arange(places, dtype=jnp.int32)[None, None, :]
    local_row = flat // col_span
    local_col = flat % col_span
    global_row = row_pos * row_span + local_row
    global_col = (local_col // SEG_T * N_COL + col_pos) * SEG_T + local_col % SEG_T
    allowed = (global_row >= global_col).astype(jnp.int32)
    usable = jnp.sum(allowed, axis=2)
    highest_use = jnp.max(usable)
    jitter = jax.random.randint(key_jitter, (N_ROW, N_COL), 0, 3)
    jitter = jnp.where(usable == highest_use, 0, jitter)
    counts = jnp.clip((usable * TILES_DEV + highest_use - 1) // highest_use - jitter, 1, TILES_DEV)
    scores = jax.random.randint(key_order, (N_ROW, N_COL, places), 0, 4096) * places + flat + allowed * (4096 * places)
    order = jnp.argsort(-scores, axis=2, stable=True)[:, :, :TILES_DEV]
    live = jnp.arange(TILES_DEV, dtype=jnp.int32)[None, None, :] < counts[:, :, None]
    rows = jnp.where(live, order // col_span, 0)
    cols = jnp.where(live, order % col_span, 0)
    return (counts.astype(jnp.int32), rows.astype(jnp.int32), cols.astype(jnp.int32))


def draw_tile_count(key, part):
    return tile_layout(key)[0]


def draw_tile_rows(key, part):
    return tile_layout(key)[1]


def draw_tile_cols(key, part):
    return tile_layout(key)[2]


def draw_tiles(key, part):
    counts, rows, cols = tile_layout(key)
    key_value = jax.random.fold_in(key, 11)
    key_diag = jax.random.fold_in(key, 12)
    shape = (N_ROW, N_COL, TILES_DEV, TILE, TILE)
    sigma = (TILE * TILES_DEV) ** (-0.5)
    values = jax.random.normal(key_value, shape, jnp.float32) * sigma
    row_pos = jnp.arange(N_ROW, dtype=jnp.int32)[:, None, None]
    col_pos = jnp.arange(N_COL, dtype=jnp.int32)[None, :, None]
    global_row = row_pos * (N_COL * SEG_T) + rows
    global_col = (cols // SEG_T * N_COL + col_pos) * SEG_T + cols % SEG_T
    live = jnp.arange(TILES_DEV, dtype=jnp.int32)[None, None, :] < counts[:, :, None]
    on_diag = jnp.logical_and(global_row == global_col, live).astype(jnp.float32)
    heights = jax.random.uniform(key_diag, (N_ROW, N_COL, TILES_DEV, 1, TILE), jnp.float32, 2.0, 6.0)
    ident = (jnp.arange(TILE)[:, None] == jnp.arange(TILE)[None, :]).astype(jnp.float32)
    return values + on_diag[:, :, :, None, None] * ident * heights


def shard_levels(stream_key, extent, cuts, low, high):
    level, own = 1.0, jax.random.fold_in(stream_key, 6)
    for axis_at, shards_of in cuts:
        draws = jnp.exp(jax.random.uniform(jax.random.fold_in(own, axis_at), (shards_of,), jnp.float32, low / len(cuts), high / len(cuts)))
        level = level * jnp.repeat(draws, extent[axis_at] // shards_of).reshape([-1 if axis == axis_at else 1 for axis in range(len(extent))])
    return level


def noise(stream_key, extent, scale, limit, cuts=(), kind=jnp.bfloat16):
    loudness = shard_levels(stream_key, extent, cuts, -0.22, 0.18) if cuts else 1.0
    drawn = jax.random.normal(stream_key, extent, jnp.float32) * scale * loudness
    return jnp.minimum(jnp.maximum(drawn, -limit), limit).astype(kind)


def setup_inputs(seed: int = 0) -> dict:
    arg_keys = jax.random.split(jax.random.key(seed), 6)
    return {
        "tile_count": draw_tile_count(jax.random.fold_in(arg_keys[5], 71), 0),
        "tile_rows": draw_tile_rows(jax.random.fold_in(arg_keys[5], 71), 0),
        "tile_cols": draw_tile_cols(jax.random.fold_in(arg_keys[5], 71), 0),
        "tiles": draw_tiles(jax.random.fold_in(arg_keys[5], 71), 0),
        "block": noise(arg_keys[4], (K, N), 1.0, 6.0, ((1, 256),), jnp.float32),
    }


highest = lax.Precision.HIGHEST


def inner_prod(left, right):
    return jnp.dot(left, right.T, precision=highest, preferred_element_type=jnp.float32)


def reference(tile_count, tile_rows, tile_cols, tiles, block):
    vec_count, total_rows = block.shape
    tile_size = tiles.shape[-1]
    tile_total = total_rows // tile_size
    row_pos = jnp.arange(N_ROW, dtype=jnp.int32)[:, None, None]
    col_pos = jnp.arange(N_COL, dtype=jnp.int32)[None, :, None]
    global_row = (row_pos * (N_COL * SEG_T) + tile_rows).astype(jnp.int32)
    global_col = (((tile_cols // SEG_T) * N_COL + col_pos) * SEG_T + tile_cols % SEG_T).astype(jnp.int32)
    slot_pos = jnp.arange(TILES_DEV, dtype=jnp.int32)[None, None, :]
    live_mask = (slot_pos < tile_count[:, :, None]).astype(jnp.float32)
    groups = N_ROW * N_COL * TILES_DEV // 64
    data_all = tiles.reshape(groups, 64, tile_size, tile_size)
    rows_all = global_row.reshape(groups, 64)
    cols_all = global_col.reshape(groups, 64)
    mask_all = live_mask.reshape(groups, 64)

    def apply_h(vectors):
        pieces = vectors.reshape(vec_count, tile_total, tile_size)

        def step(total, item):
            data, rows, cols, mask = item
            lower_part = jnp.einsum("sij,ksj->ksi", data, pieces[:, cols], precision=highest) * mask[None, :, None]
            upper_part = jnp.einsum("sij,ksi->ksj", data, pieces[:, rows], precision=highest) * mask[None, :, None]
            total = total.at[:, rows].add(lower_part)
            total = total.at[:, cols].add(upper_part)
            return total, None

        begin = jnp.zeros((vec_count, tile_total, tile_size), jnp.float32)
        result, _ = lax.scan(step, begin, (data_all, rows_all, cols_all, mask_all))
        return result.reshape(vec_count, total_rows)

    image_x = apply_h(block)
    rayleigh = inner_prod(block, image_x) / total_rows
    resid = image_x - jnp.dot(rayleigh, block, precision=highest, preferred_element_type=jnp.float32)
    image_w = apply_h(resid)
    grams = jnp.stack([rayleigh, inner_prod(block, image_w) / total_rows, inner_prod(resid, image_w) / total_rows, inner_prod(resid, resid) / total_rows])
    return image_x, image_w, grams
```

```python
import functools

import jax
import jax.numpy as jnp
from jax import lax
from jax.experimental import pallas as pl
from jax.experimental.pallas import tpu as pltpu
from jax.sharding import PartitionSpec as P

MESH = pl.DeviceIdType.MESH
HIGHEST = lax.Precision.HIGHEST
F32 = jnp.float32
BF16 = jnp.bfloat16
RING = 4
VMEM_LIMIT = 60 * 1024 * 1024


class Place:
    def __init__(self):
        row = lax.axis_index("row")
        col = lax.axis_index("col")
        self.x, self.zh = lax.div(row, RING), lax.rem(row, RING)
        self.y = lax.div(col, RING)
        rest = lax.rem(col, RING)
        self.zl, self.core = lax.div(rest, 2), lax.rem(rest, 2)
        self.row, self.col = row, col

    def turn(self, value, by):
        return lax.rem(value + by, RING)

    def row_at(self, dx=0, dz=0):
        return self.turn(self.x, dx) * RING + self.turn(self.zh, dz)

    def col_at(self, dy=0, flip_zl=False, flip_core=False):
        zl = 1 - self.zl if flip_zl else self.zl
        core = 1 - self.core if flip_core else self.core
        return (self.turn(self.y, dy) * 2 + zl) * 2 + core

    def peer(self, dx=0, dz=0, dy=0, flip_zl=False, flip_core=False):
        return (self.row_at(dx, dz), self.col_at(dy, flip_zl, flip_core))


class Wires:
    def __init__(self, place, send_sems, recv_sems):
        self.place, self.send_sems, self.recv_sems = place, send_sems, recv_sems
        self.sent = []

    def send(self, src, dst, peer):
        number = len(self.sent)
        copy = pltpu.make_async_remote_copy(
            src_ref=src,
            dst_ref=dst,
            send_sem=self.send_sems.at[number],
            recv_sem=self.recv_sems.at[number],
            device_id=peer,
            device_id_type=MESH,
        )
        copy.start()
        self.sent.append(copy)
        return number

    def arrived(self, number, landing):
        pltpu.make_async_remote_copy(
            src_ref=landing,
            dst_ref=landing,
            send_sem=self.send_sems.at[number],
            recv_sem=self.recv_sems.at[number],
            device_id=self.place.peer(flip_core=True),
            device_id_type=MESH,
        ).wait_recv()

    def drain(self):
        for copy in self.sent:
            copy.wait_send()


def greet(peers):
    barrier = pltpu.get_barrier_semaphore()
    for peer in peers:
        pl.semaphore_signal(barrier, inc=1, device_id=peer, device_id_type=MESH)
    pl.semaphore_wait(barrier, len(peers))


def near_peers(place):
    return [
        place.peer(dx=1),
        place.peer(dx=3),
        place.peer(dz=1),
        place.peer(dz=3),
        place.peer(dy=1),
        place.peer(dy=3),
        place.peer(flip_zl=True),
        place.peer(flip_core=True),
    ]


def sum_peers(place):
    return [place.peer(dx=2), place.peer(dz=2), place.peer(dy=2)]


def gather(place, wires, own, near, far):
    send, arrived = wires.send, wires.arrived

    def far_at(u, dx=0, dz=0):
        return far.at[place.row_at(dx, dz) * 2 + u]

    def near_at(u, dy=0, flip_zl=False, flip_core=False):
        return near.at[place.col_at(dy, flip_zl, flip_core) * 2 + u]

    xp, xm = place.peer(dx=1), place.peer(dx=3)
    zp, zm = place.peer(dz=1), place.peer(dz=3)
    yp, ym = place.peer(dy=1), place.peer(dy=3)
    zl_peer, core_peer = place.peer(flip_zl=True), place.peer(flip_core=True)

    zp_own, zm_own, zl_own = {}, {}, {}
    to_xp, to_xm, fwd_xp, fwd_xm = {}, {}, {}, {}
    to_yp, to_ym, fwd_yp, fwd_ym = {}, {}, {}, {}
    shared = {}

    def x_out(dz, u, src):
        to_xp[dz, u] = send(src, far_at(u, dz=dz), xp)
        to_xm[dz, u] = send(src, far_at(u, dz=dz), xm)

    def y_out(flip, u, src):
        to_yp[flip, u] = send(src, near_at(u, flip_zl=flip), yp)
        to_ym[flip, u] = send(src, near_at(u, flip_zl=flip), ym)

    def share(dy, flip, u, src):
        shared[dy, flip, u] = send(src, near_at(u, dy, flip), core_peer)

    for u in range(2):
        zl_own[u] = send(own(u), near_at(u), zl_peer)
        zp_own[u] = send(own(u), far_at(u), zp)
        zm_own[u] = send(own(u), far_at(u), zm)
        x_out(0, u, own(u))
        y_out(False, u, own(u))
        share(0, False, u, own(u))
    yield

    def x_in(dz):
        arrived(to_xp[dz, 0], far_at(0, dx=3, dz=dz))
        fwd_xp[dz] = send(far_at(0, dx=3, dz=dz), far_at(0, dx=3, dz=dz), xp)
        arrived(to_xm[dz, 1], far_at(1, dx=1, dz=dz))
        fwd_xm[dz] = send(far_at(1, dx=1, dz=dz), far_at(1, dx=1, dz=dz), xm)

    def y_in(flip):
        arrived(to_yp[flip, 0], near_at(0, 3, flip))
        fwd_yp[flip] = send(near_at(0, 3, flip), near_at(0, 3, flip), yp)
        share(3, flip, 0, near_at(0, 3, flip))
        arrived(to_ym[flip, 1], near_at(1, 1, flip))
        fwd_ym[flip] = send(near_at(1, 1, flip), near_at(1, 1, flip), ym)
        share(1, flip, 1, near_at(1, 1, flip))

    def y_rest(flip):
        arrived(to_ym[flip, 0], near_at(0, 1, flip))
        share(1, flip, 0, near_at(0, 1, flip))
        arrived(to_yp[flip, 1], near_at(1, 3, flip))
        share(3, flip, 1, near_at(1, 3, flip))

    def y_far(flip):
        arrived(fwd_yp[flip], near_at(0, 2, flip))
        share(2, flip, 0, near_at(0, 2, flip))
        arrived(fwd_ym[flip], near_at(1, 2, flip))
        share(2, flip, 1, near_at(1, 2, flip))

    for u in range(2):
        arrived(zl_own[u], near_at(u, flip_zl=True))
        y_out(True, u, near_at(u, flip_zl=True))
        share(0, True, u, near_at(u, flip_zl=True))
    x_in(0)
    y_in(False)
    arrived(zp_own[0], far_at(0, dz=3))
    fwd_zp = send(far_at(0, dz=3), far_at(0, dz=3), zp)
    x_out(3, 0, far_at(0, dz=3))
    arrived(zm_own[0], far_at(0, dz=1))
    x_out(1, 0, far_at(0, dz=1))
    arrived(zm_own[1], far_at(1, dz=1))
    fwd_zm = send(far_at(1, dz=1), far_at(1, dz=1), zm)
    x_out(1, 1, far_at(1, dz=1))
    arrived(zp_own[1], far_at(1, dz=3))
    x_out(3, 1, far_at(1, dz=3))
    y_rest(False)
    y_in(True)
    arrived(fwd_zp, far_at(0, dz=2))
    x_out(2, 0, far_at(0, dz=2))
    arrived(fwd_zm, far_at(1, dz=2))
    x_out(2, 1, far_at(1, dz=2))
    x_in(3)
    x_in(1)
    y_far(False)
    y_rest(True)
    y_far(True)
    x_in(2)
    for dz in (0, 3, 1, 2):
        arrived(to_xm[dz, 0], far_at(0, dx=1, dz=dz))
        arrived(to_xp[dz, 1], far_at(1, dx=3, dz=dz))
        arrived(fwd_xp[dz], far_at(0, dx=2, dz=dz))
        arrived(fwd_xm[dz], far_at(1, dx=2, dz=dz))
    for (dy, flip, u), number in shared.items():
        arrived(number, near_at(u, dy, flip, True))
    yield


class RingSum:
    def __init__(self, wires, term, box, pair, plus, minus):
        self.wires, self.term, self.box, self.pair = wires, term, box, pair
        self.plus, self.minus = plus, minus

    def opposite(self):
        send = self.wires.send
        self.opp = (
            send(self.term(2, 0), self.box(0), self.plus),
            send(self.term(2, 1), self.box(1), self.minus),
        )

    def plain(self):
        send = self.wires.send
        self.flat = (
            send(self.term(1, 1), self.box(2), self.plus),
            send(self.term(3, 0), self.box(3), self.minus),
        )

    def joined(self):
        send, arrived = self.wires.send, self.wires.arrived
        arrived(self.opp[0], self.box(0))
        self.pair(0)[...] = self.term(1, 0)[...] + self.box(0)[...]
        first = send(self.pair(0), self.box(4), self.plus)
        arrived(self.opp[1], self.box(1))
        self.pair(1)[...] = self.term(3, 1)[...] + self.box(1)[...]
        second = send(self.pair(1), self.box(5), self.minus)
        self.both = (first, second)

    def total(self):
        arrived = self.wires.arrived
        arrived(self.flat[0], self.box(2))
        arrived(self.flat[1], self.box(3))
        arrived(self.both[0], self.box(4))
        arrived(self.both[1], self.box(5))
        low = self.term(0, 0)[...] + (self.box(4)[...] + self.box(3)[...])
        high = self.term(0, 1)[...] + (self.box(2)[...] + self.box(5)[...])
        return low, high


class SmallSum:
    def __init__(self, place, wires, slots):
        self.place, self.wires, self.slots = place, wires, slots

    def pair_out(self, stage, value, mine, peer):
        self.mine = mine
        self.slots[stage, mine] = value
        self.numbers = [self.wires.send(self.slots.at[stage, mine], self.slots.at[stage, mine], peer)]

    def pair_in(self, stage):
        self.wires.arrived(self.numbers[0], self.slots.at[stage, 1 - self.mine])
        return self.slots[stage, 0] + self.slots[stage, 1]

    def ring_out(self, stage, value, mine, peers):
        self.mine = mine
        self.slots[stage, mine] = value
        self.numbers = [
            self.wires.send(self.slots.at[stage, mine], self.slots.at[stage, mine], peers[by])
            for by in (1, 2, 3)
        ]

    def ring_in(self, stage):
        for number, by in zip(self.numbers, (1, 2, 3)):
            origin = lax.rem(self.mine + RING - by, RING)
            self.wires.arrived(number, self.slots.at[stage, origin])
        return (self.slots[stage, 0] + self.slots[stage, 1]) + (self.slots[stage, 2] + self.slots[stage, 3])

    def run(self, value):
        place = self.place
        self.pair_out(0, value, place.core, place.peer(flip_core=True))
        yield None
        value = self.pair_in(0)
        self.pair_out(1, value, place.zl, place.peer(flip_zl=True))
        yield None
        value = self.pair_in(1)
        self.ring_out(2, value, place.y, {by: place.peer(dy=by) for by in (1, 2, 3)})
        yield None
        value = self.ring_in(2)
        self.ring_out(3, value, place.x, {by: place.peer(dx=by) for by in (1, 2, 3)})
        yield None
        value = self.ring_in(3)
        self.ring_out(4, value, place.zh, {by: place.peer(dz=by) for by in (1, 2, 3)})
        yield None
        yield self.ring_in(4)


def reduce_all(place, wires, small, part_rows, part_cols, boxes, make_small):
    core_box, near_sum, y_box, y_pair, y_held, zl_box, x_box, x_pair, x_held, z_box, z_pair = boxes
    send, arrived = wires.send, wires.arrived
    xp, xm = place.peer(dx=1), place.peer(dx=3)
    zp, zm = place.peer(dz=1), place.peer(dz=3)
    yp, ym = place.peer(dy=1), place.peer(dy=3)
    zl_peer, core_peer = place.peer(flip_zl=True), place.peer(flip_core=True)

    def x_ring(k, dz):
        return RingSum(
            wires,
            lambda d, u: part_cols.at[place.row_at(d, dz) * 2 + u],
            lambda i: x_box.at[k, i],
            lambda i: x_pair.at[k, i],
            xp,
            xm,
        )

    depths = (2, 1, 3, 0)
    x_rings = [x_ring(k, dz) for k, dz in enumerate(depths)]
    crossed = {}
    x_rings[0].opposite()
    x_rings[1].opposite()
    for dy in (2, 1, 3, 0):
        for flip in (True, False):
            source = place.col_at(dy, flip, True) * 2
            crossed[dy, flip] = send(
                part_rows.at[pl.ds(source, 2)], core_box.at[dy, int(flip)], core_peer
            )
    x_rings[0].plain()
    sums = small.run(make_small())
    next(sums)

    def y_ring(flip):
        return RingSum(
            wires,
            lambda d, u: near_sum.at[d, int(flip), u],
            lambda i: y_box.at[int(flip), i],
            lambda i: y_pair.at[int(flip), i],
            yp,
            ym,
        )

    y_rings = {flip: y_ring(flip) for flip in (True, False)}

    def cross(dy, flip):
        arrived(crossed[dy, flip], core_box.at[dy, int(flip)])
        source = place.col_at(dy, flip) * 2
        near_sum[dy, int(flip)] = part_rows[pl.ds(source, 2)] + core_box[dy, int(flip)]

    for flip in (True, False):
        cross(2, flip)
        y_rings[flip].opposite()
    x_rings[0].joined()
    x_rings[2].opposite()
    x_rings[1].plain()
    for flip in (True, False):
        cross(1, flip)
        cross(3, flip)
        y_rings[flip].plain()
    next(sums)
    x_rings[1].joined()
    x_rings[3].opposite()
    x_rings[2].plain()
    y_rings[True].joined()
    for flip in (True, False):
        cross(0, flip)
    next(sums)
    y_rings[False].joined()

    def hold_x(k):
        x_held[k, 0], x_held[k, 1] = x_rings[k].total()

    z_ring = RingSum(
        wires,
        lambda d, u: x_held.at[depths.index(d), u],
        lambda i: z_box.at[i],
        lambda i: z_pair.at[i],
        zp,
        zm,
    )
    hold_x(0)
    z_ring.opposite()
    x_rings[2].joined()
    x_rings[3].plain()
    next(sums)
    y_held[1, 0], y_held[1, 1] = y_rings[True].total()
    zl_sent = send(y_held.at[1], zl_box, zl_peer)
    x_rings[3].joined()
    y_held[0, 0], y_held[0, 1] = y_rings[False].total()
    hold_x(1)
    hold_x(2)
    z_ring.plain()
    next(sums)
    z_ring.joined()
    arrived(zl_sent, zl_box)
    small_total = next(sums)
    hold_x(3)
    low, high = z_ring.total()
    halves = (
        low + (y_held[0, 0] + zl_box[0]),
        high + (y_held[0, 1] + zl_box[1]),
    )
    return halves, small_total


def reduce_scratch(K, T, rows):
    return [
        pltpu.VMEM((4, 2, 2, K, T), F32),
        pltpu.VMEM((4, 2, 2, K, T), F32),
        pltpu.VMEM((2, 6, K, T), F32),
        pltpu.VMEM((2, 2, K, T), F32),
        pltpu.VMEM((2, 2, K, T), F32),
        pltpu.VMEM((2, K, T), F32),
        pltpu.VMEM((4, 6, K, T), F32),
        pltpu.VMEM((4, 2, K, T), F32),
        pltpu.VMEM((4, 2, K, T), F32),
        pltpu.VMEM((6, K, T), F32),
        pltpu.VMEM((2, K, T), F32),
        pltpu.VMEM((5, 4, rows, 2 * K), F32),
    ]


def split(value):
    high = value.astype(BF16)
    low = (value - high.astype(F32)).astype(BF16)
    return high, low


def dot_t(left, right, precision=None):
    return lax.dot_general(
        left, right, (((1,), (1,)), ((), ())), precision=precision, preferred_element_type=F32
    )


def dot_n(left, right, precision=None):
    return lax.dot_general(
        left, right, (((1,), (0,)), ((), ())), precision=precision, preferred_element_type=F32
    )


def fold(square):
    half = square.shape[0] // 2
    return jnp.concatenate([square[:half], square[half:]], axis=1)


def unfold(flat):
    half = flat.shape[1] // 2
    return jnp.concatenate([flat[:, :half], flat[:, half:]], axis=0)


def energy(part_rows, near):
    K = part_rows.shape[1]

    def step(p, total):
        left = jnp.concatenate(split(part_rows[p]), axis=0)
        right = jnp.concatenate(split(near[p]), axis=0)
        return total + dot_t(left, right)

    total = lax.fori_loop(0, part_rows.shape[0], step, jnp.zeros((2 * K, 2 * K), F32))
    total = total[:K] + total[K:]
    total = total[:, :K] + total[:, K:]
    return total + total.T


def first_kernel(block, near, far, send_sems, recv_sems):
    place = Place()
    K, width = block.shape
    T = width // 2
    greet(near_peers(place))
    wires = Wires(place, send_sems, recv_sems)
    steps = gather(place, wires, lambda u: block.at[:, pl.ds(u * T, T)], near, far)
    next(steps)
    for u in range(2):
        half = block[:, u * T : (u + 1) * T]
        near[place.col * 2 + u] = half
        far[place.row * 2 + u] = half
    next(steps)
    wires.drain()


def middle_kernel(
    total_rows, block, near_x, part_rows, part_cols, image, rayleigh, grams, near, far, *scratch
):
    *boxes, slots, resid, send_sems, recv_sems = scratch
    place = Place()
    K, width = block.shape
    T = width // 2
    greet(near_peers(place) + sum_peers(place))
    wires = Wires(place, send_sems, recv_sems)
    small = SmallSum(place, wires, slots)
    halves, total = reduce_all(
        place, wires, small, part_rows, part_cols, boxes, lambda: fold(energy(part_rows, near_x))
    )
    mean = unfold(total) / total_rows
    for u in range(2):
        resid[u] = halves[u] - dot_n(mean, block[:, u * T : (u + 1) * T], HIGHEST)
    steps = gather(place, wires, lambda u: resid.at[u], near, far)
    next(steps)
    rayleigh[...] = mean
    cross = jnp.zeros((K, K), F32)
    square = jnp.zeros((K, K), F32)
    for u in range(2):
        image[:, u * T : (u + 1) * T] = halves[u]
        value = resid[u]
        near[place.col * 2 + u] = value
        far[place.row * 2 + u] = value
        cross += dot_t(halves[u], value, HIGHEST)
        square += dot_t(value, value, HIGHEST)
    grams[0] = cross
    grams[1] = square
    next(steps)
    wires.drain()


def last_kernel(
    total_rows, rayleigh, local_grams, near_w, part_rows, part_cols, image, grams, *scratch
):
    *boxes, slots, send_sems, recv_sems = scratch
    place = Place()
    T = part_rows.shape[2]
    half = rayleigh.shape[0] // 2
    greet(near_peers(place) + sum_peers(place))
    wires = Wires(place, send_sems, recv_sems)
    small = SmallSum(place, wires, slots)

    def make_small():
        return jnp.concatenate(
            [
                fold(local_grams[0]),
                fold(energy(part_rows, near_w)),
                fold(local_grams[1]),
            ],
            axis=0,
        )

    halves, total = reduce_all(place, wires, small, part_rows, part_cols, boxes, make_small)
    for u in range(2):
        image[:, u * T : (u + 1) * T] = halves[u]
    grams[0] = rayleigh[...]
    for i in range(3):
        grams[1 + i] = unfold(total[i * half : (i + 1) * half]) / total_rows
    wires.drain()


def tile_kernel(
    count, row_ids, col_ids, tiles, near, far, part_rows, part_cols, held, near_two, far_two, sems
):
    slots = tiles.shape[0]
    live = count[0]

    def fetch(s):
        return pltpu.make_async_copy(tiles.at[s], held.at[s], sems.at[s])

    for s in range(slots):
        fetch(s).start()
    zero = jnp.zeros(part_rows.shape[1:], F32)

    def prepare(p, carry):
        part_rows[p] = zero
        part_cols[p] = zero
        near_two[p] = jnp.concatenate(split(near[p]), axis=0)
        far_two[p] = jnp.concatenate(split(far[p]), axis=0)
        return carry

    lax.fori_loop(0, part_rows.shape[0], prepare, 0)
    K = near.shape[1]

    def step(s, carry):
        fetch(s).wait()
        row, col = row_ids[s], col_ids[s]
        high, low = split(held[s])
        rows_in, cols_in = near_two[row], far_two[col]
        lower = dot_t(cols_in, high)
        upper = dot_n(rows_in, high)
        part_rows[row] += (lower[:K] + lower[K:]) + dot_t(cols_in[:K], low)
        part_cols[col] += (upper[:K] + upper[K:]) + dot_n(rows_in[:K], low)
        return carry

    lax.fori_loop(0, live, step, 0)

    def finish(s, carry):
        fetch(s).wait()
        return carry

    lax.fori_loop(live, slots, finish, 0)


def vmem(count):
    return [pl.BlockSpec(memory_space=pltpu.VMEM)] * count


def on_device(tile_count, tile_rows, tile_cols, tiles, block):
    K, width = block.shape
    T = tiles.shape[-1]
    slots = tiles.shape[2]
    total_rows = width * lax.axis_size("row") * lax.axis_size("col")
    count, row_ids, col_ids = tile_count[0], tile_rows[0, 0], tile_cols[0, 0]
    data = tiles[0, 0]
    strip = jax.ShapeDtypeStruct((32, K, T), F32)
    seg = jax.ShapeDtypeStruct((K, width), F32)

    def params(number):
        return pltpu.CompilerParams(
            collective_id=number, has_side_effects=True, vmem_limit_bytes=VMEM_LIMIT
        )

    def sems(count):
        return [pltpu.SemaphoreType.DMA((count,)), pltpu.SemaphoreType.DMA((count,))]

    near, far = pl.pallas_call(
        first_kernel,
        out_shape=(strip, strip),
        in_specs=vmem(1),
        out_specs=tuple(vmem(2)),
        scratch_shapes=sems(60),
        compiler_params=params(0),
        name="gather_block",
    )(block)

    def products(near, far):
        smem = pl.BlockSpec(memory_space=pltpu.SMEM)
        return pl.pallas_call(
            tile_kernel,
            out_shape=(strip, strip),
            in_specs=[smem, smem, smem, pl.BlockSpec(memory_space=pl.ANY)] + vmem(2),
            out_specs=tuple(vmem(2)),
            scratch_shapes=[
                pltpu.VMEM((slots, T, T), F32),
                pltpu.VMEM((32, 2 * K, T), BF16),
                pltpu.VMEM((32, 2 * K, T), BF16),
                pltpu.SemaphoreType.DMA((slots,)),
            ],
            compiler_params=pltpu.CompilerParams(vmem_limit_bytes=VMEM_LIMIT),
            name="tile_products",
        )(count, row_ids, col_ids, data, near, far)

    part_rows, part_cols = products(near, far)
    image_x, rayleigh, local_grams, near_w, far_w = pl.pallas_call(
        functools.partial(middle_kernel, total_rows),
        out_shape=(
            seg,
            jax.ShapeDtypeStruct((K, K), F32),
            jax.ShapeDtypeStruct((2, K, K), F32),
            strip,
            strip,
        ),
        in_specs=vmem(4),
        out_specs=tuple(vmem(5)),
        scratch_shapes=reduce_scratch(K, T, K // 2) + [pltpu.VMEM((2, K, T), F32)] + sems(136),
        compiler_params=params(1),
        name="reduce_and_gather",
    )(block, near, part_rows, part_cols)
    part_rows, part_cols = products(near_w, far_w)
    image_w, grams = pl.pallas_call(
        functools.partial(last_kernel, total_rows),
        out_shape=(seg, jax.ShapeDtypeStruct((4, K, K), F32)),
        in_specs=vmem(5),
        out_specs=tuple(vmem(2)),
        scratch_shapes=reduce_scratch(K, T, 3 * K // 2) + sems(76),
        compiler_params=params(2),
        name="reduce_last",
    )(rayleigh, local_grams, near_w, part_rows, part_cols)
    return image_x, image_w, grams


def solution(mesh):
    return jax.shard_map(
        on_device,
        mesh=mesh,
        in_specs=(
            P("row", "col"),
            P("row", "col", None),
            P("row", "col", None),
            P("row", "col", None, None, None),
            P(None, ("row", "col")),
        ),
        out_specs=(P(None, ("row", "col")), P(None, ("row", "col")), P()),
        check_vma=False,
    )
```

```python
import functools

import jax
import jax.numpy as jnp
from jax import lax
from jax.experimental import pallas as pl
from jax.experimental.pallas import tpu as pltpu
from jax.sharding import PartitionSpec as P

MESH = pl.DeviceIdType.MESH
HIGHEST = lax.Precision.HIGHEST
F32 = jnp.float32
BF16 = jnp.bfloat16
RING = 4
VMEM_LIMIT = 60 * 1024 * 1024


class Place:
    def __init__(self):
        row = lax.axis_index("row")
        col = lax.axis_index("col")
        self.x, self.zh = lax.div(row, RING), lax.rem(row, RING)
        self.y = lax.div(col, RING)
        rest = lax.rem(col, RING)
        self.zl, self.core = lax.div(rest, 2), lax.rem(rest, 2)
        self.row, self.col = row, col

    def turn(self, value, by):
        return lax.rem(value + by, RING)

    def row_at(self, dx=0, dz=0):
        return self.turn(self.x, dx) * RING + self.turn(self.zh, dz)

    def col_at(self, dy=0, flip_zl=False, flip_core=False):
        zl = 1 - self.zl if flip_zl else self.zl
        core = 1 - self.core if flip_core else self.core
        return (self.turn(self.y, dy) * 2 + zl) * 2 + core

    def peer(self, dx=0, dz=0, dy=0, flip_zl=False, flip_core=False):
        return (self.row_at(dx, dz), self.col_at(dy, flip_zl, flip_core))


class Wires:
    def __init__(self, place, send_sems, recv_sems):
        self.place, self.send_sems, self.recv_sems = place, send_sems, recv_sems
        self.sent = []

    def send(self, src, dst, peer):
        number = len(self.sent)
        copy = pltpu.make_async_remote_copy(
            src_ref=src,
            dst_ref=dst,
            send_sem=self.send_sems.at[number],
            recv_sem=self.recv_sems.at[number],
            device_id=peer,
            device_id_type=MESH,
        )
        copy.start()
        self.sent.append(copy)
        return number

    def arrived(self, number, landing):
        pltpu.make_async_remote_copy(
            src_ref=landing,
            dst_ref=landing,
            send_sem=self.send_sems.at[number],
            recv_sem=self.recv_sems.at[number],
            device_id=self.place.peer(flip_core=True),
            device_id_type=MESH,
        ).wait_recv()

    def drain(self):
        for copy in self.sent:
            copy.wait_send()


def greet(peers):
    barrier = pltpu.get_barrier_semaphore()
    for peer in peers:
        pl.semaphore_signal(barrier, inc=1, device_id=peer, device_id_type=MESH)
    pl.semaphore_wait(barrier, len(peers))


def near_peers(place):
    return [
        place.peer(dx=1),
        place.peer(dx=3),
        place.peer(dz=1),
        place.peer(dz=3),
        place.peer(dy=1),
        place.peer(dy=3),
        place.peer(flip_zl=True),
        place.peer(flip_core=True),
    ]


def sum_peers(place):
    return [place.peer(dx=2), place.peer(dz=2), place.peer(dy=2)]


def gather(place, wires, own, near, far):
    send, arrived = wires.send, wires.arrived

    def far_at(u, dx=0, dz=0):
        return far.at[place.row_at(dx, dz) * 2 + u]

    def near_at(u, dy=0, flip_zl=False, flip_core=False):
        return near.at[place.col_at(dy, flip_zl, flip_core) * 2 + u]

    xp, xm = place.peer(dx=1), place.peer(dx=3)
    zp, zm = place.peer(dz=1), place.peer(dz=3)
    yp, ym = place.peer(dy=1), place.peer(dy=3)
    zl_peer, core_peer = place.peer(flip_zl=True), place.peer(flip_core=True)

    zp_own, zm_own, zl_own = {}, {}, {}
    to_xp, to_xm, fwd_xp, fwd_xm = {}, {}, {}, {}
    to_yp, to_ym, fwd_yp, fwd_ym = {}, {}, {}, {}
    shared = {}

    def x_out(dz, u, src):
        to_xp[dz, u] = send(src, far_at(u, dz=dz), xp)
        to_xm[dz, u] = send(src, far_at(u, dz=dz), xm)

    def y_out(flip, u, src):
        to_yp[flip, u] = send(src, near_at(u, flip_zl=flip), yp)
        to_ym[flip, u] = send(src, near_at(u, flip_zl=flip), ym)

    def share(dy, flip, u, src):
        shared[dy, flip, u] = send(src, near_at(u, dy, flip), core_peer)

    for u in range(2):
        zl_own[u] = send(own(u), near_at(u), zl_peer)
    for u in range(2):
        zp_own[u] = send(own(u), far_at(u), zp)
        zm_own[u] = send(own(u), far_at(u), zm)
        x_out(0, u, own(u))
        y_out(False, u, own(u))
    for u in range(2):
        share(0, False, u, own(u))
    yield

    def x_in(dz):
        arrived(to_xp[dz, 0], far_at(0, dx=3, dz=dz))
        fwd_xp[dz] = send(far_at(0, dx=3, dz=dz), far_at(0, dx=3, dz=dz), xp)
        arrived(to_xm[dz, 1], far_at(1, dx=1, dz=dz))
        fwd_xm[dz] = send(far_at(1, dx=1, dz=dz), far_at(1, dx=1, dz=dz), xm)

    def y_in(flip):
        arrived(to_yp[flip, 0], near_at(0, 3, flip))
        fwd_yp[flip] = send(near_at(0, 3, flip), near_at(0, 3, flip), yp)
        share(3, flip, 0, near_at(0, 3, flip))
        arrived(to_ym[flip, 1], near_at(1, 1, flip))
        fwd_ym[flip] = send(near_at(1, 1, flip), near_at(1, 1, flip), ym)
        share(1, flip, 1, near_at(1, 1, flip))

    def y_rest(flip):
        arrived(to_ym[flip, 0], near_at(0, 1, flip))
        share(1, flip, 0, near_at(0, 1, flip))
        arrived(to_yp[flip, 1], near_at(1, 3, flip))
        share(3, flip, 1, near_at(1, 3, flip))

    def y_far(flip):
        arrived(fwd_yp[flip], near_at(0, 2, flip))
        share(2, flip, 0, near_at(0, 2, flip))
        arrived(fwd_ym[flip], near_at(1, 2, flip))
        share(2, flip, 1, near_at(1, 2, flip))

    for u in range(2):
        arrived(zl_own[u], near_at(u, flip_zl=True))
        y_out(True, u, near_at(u, flip_zl=True))
        share(0, True, u, near_at(u, flip_zl=True))
    yield
    x_in(0)
    y_in(False)
    arrived(zp_own[0], far_at(0, dz=3))
    fwd_zp = send(far_at(0, dz=3), far_at(0, dz=3), zp)
    x_out(3, 0, far_at(0, dz=3))
    arrived(zm_own[1], far_at(1, dz=1))
    fwd_zm = send(far_at(1, dz=1), far_at(1, dz=1), zm)
    x_out(1, 1, far_at(1, dz=1))
    yield
    arrived(zm_own[0], far_at(0, dz=1))
    x_out(1, 0, far_at(0, dz=1))
    arrived(zp_own[1], far_at(1, dz=3))
    x_out(3, 1, far_at(1, dz=3))
    y_rest(False)
    y_in(True)
    yield
    y_far(False)
    y_rest(True)
    arrived(fwd_zp, far_at(0, dz=2))
    x_out(2, 0, far_at(0, dz=2))
    arrived(fwd_zm, far_at(1, dz=2))
    x_out(2, 1, far_at(1, dz=2))
    x_in(3)
    yield
    x_in(1)
    y_far(True)
    for (dy, flip, u), number in shared.items():
        arrived(number, near_at(u, dy, flip, True))
    yield "near"
    x_in(2)
    yield
    for dz in (0, 3, 1, 2):
        arrived(to_xm[dz, 0], far_at(0, dx=1, dz=dz))
        arrived(to_xp[dz, 1], far_at(1, dx=3, dz=dz))
        arrived(fwd_xp[dz], far_at(0, dx=2, dz=dz))
        arrived(fwd_xm[dz], far_at(1, dx=2, dz=dz))
    yield "far"


class RingSum:
    def __init__(self, wires, term, box, pair, plus, minus):
        self.wires, self.term, self.box, self.pair = wires, term, box, pair
        self.plus, self.minus = plus, minus

    def opposite(self):
        send = self.wires.send
        self.opp = (
            send(self.term(2, 0), self.box(0), self.plus),
            send(self.term(2, 1), self.box(1), self.minus),
        )

    def plain(self):
        send = self.wires.send
        self.flat = (
            send(self.term(1, 1), self.box(2), self.plus),
            send(self.term(3, 0), self.box(3), self.minus),
        )

    def joined(self):
        send, arrived = self.wires.send, self.wires.arrived
        arrived(self.opp[0], self.box(0))
        self.pair(0)[...] = self.term(1, 0)[...] + self.box(0)[...]
        first = send(self.pair(0), self.box(4), self.plus)
        arrived(self.opp[1], self.box(1))
        self.pair(1)[...] = self.term(3, 1)[...] + self.box(1)[...]
        second = send(self.pair(1), self.box(5), self.minus)
        self.both = (first, second)

    def total(self):
        arrived = self.wires.arrived
        arrived(self.flat[0], self.box(2))
        arrived(self.flat[1], self.box(3))
        arrived(self.both[0], self.box(4))
        arrived(self.both[1], self.box(5))
        low = self.term(0, 0)[...] + (self.box(4)[...] + self.box(3)[...])
        high = self.term(0, 1)[...] + (self.box(2)[...] + self.box(5)[...])
        return low, high


class SmallSum:
    def __init__(self, place, wires, slots):
        self.place, self.wires, self.slots = place, wires, slots

    def pair_out(self, stage, value, mine, peer):
        self.mine = mine
        self.slots[stage, mine] = value
        self.numbers = [self.wires.send(self.slots.at[stage, mine], self.slots.at[stage, mine], peer)]

    def pair_in(self, stage):
        self.wires.arrived(self.numbers[0], self.slots.at[stage, 1 - self.mine])
        return self.slots[stage, 0] + self.slots[stage, 1]

    def ring_out(self, stage, value, mine, peers):
        self.mine = mine
        self.slots[stage, mine] = value
        self.numbers = [
            self.wires.send(self.slots.at[stage, mine], self.slots.at[stage, mine], peers[by])
            for by in (1, 2, 3)
        ]

    def ring_in(self, stage):
        for number, by in zip(self.numbers, (1, 2, 3)):
            origin = lax.rem(self.mine + RING - by, RING)
            self.wires.arrived(number, self.slots.at[stage, origin])
        return (self.slots[stage, 0] + self.slots[stage, 1]) + (self.slots[stage, 2] + self.slots[stage, 3])

    def run(self, value):
        place = self.place
        self.pair_out(0, value, place.core, place.peer(flip_core=True))
        yield None
        value = self.pair_in(0)
        self.pair_out(1, value, place.zl, place.peer(flip_zl=True))
        yield None
        value = self.pair_in(1)
        self.ring_out(2, value, place.y, {by: place.peer(dy=by) for by in (1, 2, 3)})
        yield None
        value = self.ring_in(2)
        self.ring_out(3, value, place.x, {by: place.peer(dx=by) for by in (1, 2, 3)})
        yield None
        value = self.ring_in(3)
        self.ring_out(4, value, place.zh, {by: place.peer(dz=by) for by in (1, 2, 3)})
        yield None
        yield self.ring_in(4)


class Reduction:
    depths = (2, 1, 3, 0)

    def __init__(self, place, wires, part_rows, part_cols, boxes):
        self.place, self.wires = place, wires
        self.part_rows = part_rows
        (
            self.core_box,
            self.near_sum,
            y_box,
            y_pair,
            self.y_held,
            self.zl_box,
            x_box,
            x_pair,
            self.x_held,
            z_box,
            z_pair,
        ) = boxes
        xp, xm = place.peer(dx=1), place.peer(dx=3)
        zp, zm = place.peer(dz=1), place.peer(dz=3)
        yp, ym = place.peer(dy=1), place.peer(dy=3)
        self.zl_peer = place.peer(flip_zl=True)
        self.core_peer = place.peer(flip_core=True)

        def x_ring(k, dz):
            return RingSum(
                wires,
                lambda d, u: part_cols.at[place.row_at(d, dz) * 2 + u],
                lambda i: x_box.at[k, i],
                lambda i: x_pair.at[k, i],
                xp,
                xm,
            )

        def y_ring(flip):
            return RingSum(
                wires,
                lambda d, u: self.near_sum.at[d, int(flip), u],
                lambda i: y_box.at[int(flip), i],
                lambda i: y_pair.at[int(flip), i],
                yp,
                ym,
            )

        self.x = [x_ring(k, dz) for k, dz in enumerate(self.depths)]
        self.y = {flip: y_ring(flip) for flip in (True, False)}
        self.z = RingSum(
            wires,
            lambda d, u: self.x_held.at[self.depths.index(d), u],
            lambda i: z_box.at[i],
            lambda i: z_pair.at[i],
            zp,
            zm,
        )

    def cross_out(self):
        self.crossed = {}
        for dy in (2, 1, 3, 0):
            for flip in (True, False):
                source = self.place.col_at(dy, flip, True) * 2
                self.crossed[dy, flip] = self.wires.send(
                    self.part_rows.at[pl.ds(source, 2)],
                    self.core_box.at[dy, int(flip)],
                    self.core_peer,
                )

    def cross_in(self, dy, flip):
        self.wires.arrived(self.crossed[dy, flip], self.core_box.at[dy, int(flip)])
        source = self.place.col_at(dy, flip) * 2
        self.near_sum[dy, int(flip)] = self.part_rows[pl.ds(source, 2)] + self.core_box[dy, int(flip)]

    def hold_x(self, k):
        self.x_held[k, 0], self.x_held[k, 1] = self.x[k].total()

    def hold_y(self, flip):
        self.y_held[int(flip), 0], self.y_held[int(flip), 1] = self.y[flip].total()

    def zl_out(self):
        self.zl_sent = self.wires.send(self.y_held.at[1], self.zl_box, self.zl_peer)

    def finish(self):
        self.wires.arrived(self.zl_sent, self.zl_box)
        near = [self.y_held[0, u] + self.zl_box[u] for u in range(2)]
        low, high = self.z.total()
        return low + near[0], high + near[1]


def reduce_scratch(K, T):
    return [
        pltpu.VMEM((4, 2, 2, K, T), F32),
        pltpu.VMEM((4, 2, 2, K, T), F32),
        pltpu.VMEM((2, 6, K, T), F32),
        pltpu.VMEM((2, 2, K, T), F32),
        pltpu.VMEM((2, 2, K, T), F32),
        pltpu.VMEM((2, K, T), F32),
        pltpu.VMEM((4, 6, K, T), F32),
        pltpu.VMEM((4, 2, K, T), F32),
        pltpu.VMEM((4, 2, K, T), F32),
        pltpu.VMEM((6, K, T), F32),
        pltpu.VMEM((2, K, T), F32),
    ]


def split(value):
    high = value.astype(BF16)
    low = (value - high.astype(F32)).astype(BF16)
    return high, low


def dot_t(left, right, precision=None):
    return lax.dot_general(
        left, right, (((1,), (1,)), ((), ())), precision=precision, preferred_element_type=F32
    )


def dot_n(left, right, precision=None):
    return lax.dot_general(
        left, right, (((1,), (0,)), ((), ())), precision=precision, preferred_element_type=F32
    )


def fold(square):
    half = square.shape[0] // 2
    return jnp.concatenate([square[:half], square[half:]], axis=1)


def unfold(flat):
    half = flat.shape[1] // 2
    return jnp.concatenate([flat[:, :half], flat[:, half:]], axis=0)


def energy(part_rows, near):
    K = part_rows.shape[1]

    def step(p, total):
        left = jnp.concatenate(split(part_rows[p]), axis=0)
        right = jnp.concatenate(split(near[p]), axis=0)
        return total + dot_t(left, right)

    total = lax.fori_loop(0, part_rows.shape[0], step, jnp.zeros((2 * K, 2 * K), F32))
    total = total[:K] + total[K:]
    total = total[:, :K] + total[:, K:]
    return total + total.T


class Application:
    def __init__(self, place, wires, table, pairs, sums, near, far, part_rows, part_cols, boxes, slots):
        self.place, self.wires, self.table, self.pairs, self.sums = place, wires, table, pairs, sums
        self.near, self.far = near, far
        self.part_rows, self.part_cols = part_rows, part_cols
        self.slots = slots
        self.reduction = Reduction(place, wires, part_rows, part_cols, boxes)

    def upper(self, start, stop):
        K = self.near.shape[1]

        def step(s, carry):
            high, low = split(self.near[self.table[0, s]])
            both = dot_n(jnp.concatenate([high, low], axis=0), self.pairs[s, 0])
            value = (both[:K] + both[K:]) + dot_n(high, self.pairs[s, 1])
            self.sums[s + 1] = value + self.sums[self.table[3, s]]
            return carry

        lax.fori_loop(start, stop, step, 0)

    def lower(self, start, stop):
        K = self.near.shape[1]

        def step(s, carry):
            high, low = split(self.far[self.table[1, s]])
            both = dot_t(jnp.concatenate([high, low], axis=0), self.pairs[s, 0])
            value = (both[:K] + both[K:]) + dot_t(high, self.pairs[s, 1])
            self.sums[s + 1] = value + self.sums[self.table[2, s]]
            return carry

        lax.fori_loop(start, stop, step, 0)

    def collect(self, line, parts):
        def step(p, carry):
            parts[p] = self.sums[self.table[line, p]]
            return carry

        lax.fori_loop(0, parts.shape[0], step, 0)

    def run(self, own, place_own, between, make_small):
        count = self.pairs.shape[0]
        eighth = count // 5
        red = self.reduction
        between = iter(between)
        steps = gather(self.place, self.wires, own, self.near, self.far)
        next(steps)
        place_own()
        next(between, None)
        while next(steps) != "near":
            next(between, None)
        self.upper(0, 2 * eighth)
        next(steps)
        self.upper(2 * eighth, count)
        self.collect(5, self.part_cols)
        red.x[0].opposite()
        red.x[1].opposite()
        red.x[0].plain()
        next(steps)
        small = SmallSum(self.place, self.wires, self.slots).run(
            make_small(energy(self.part_cols, self.far))
        )
        next(small)
        self.lower(0, eighth)
        red.x[0].joined()
        red.x[2].opposite()
        red.x[1].plain()
        self.lower(eighth, 2 * eighth)
        next(small)
        red.x[1].joined()
        red.x[3].opposite()
        self.lower(2 * eighth, 3 * eighth)
        red.x[2].plain()
        next(small)
        self.lower(3 * eighth, 4 * eighth)
        red.x[2].joined()
        red.x[3].plain()
        self.lower(4 * eighth, count)
        self.collect(4, self.part_rows)
        red.cross_out()
        next(small)
        red.hold_x(0)
        red.z.opposite()
        for flip in (True, False):
            red.cross_in(2, flip)
            red.y[flip].opposite()
        for flip in (True, False):
            red.cross_in(1, flip)
            red.cross_in(3, flip)
            red.y[flip].plain()
        red.x[3].joined()
        next(small)
        red.cross_in(0, True)
        red.cross_in(0, False)
        red.y[True].joined()
        red.y[False].joined()
        red.hold_x(1)
        red.hold_x(2)
        red.z.plain()
        red.z.joined()
        total = next(small)
        red.hold_y(True)
        red.zl_out()
        red.hold_y(False)
        red.hold_x(3)
        return red.finish(), total


def whole_kernel(total_rows, table, tiles, block, image_x, image_w, grams, *scratch):
    (stage, stage_sems, pairs, sums, resid, send_sems, recv_sems), scratch = scratch[:7], scratch[7:]
    sets = scratch[: len(scratch) // 2], scratch[len(scratch) // 2 :]
    place = Place()
    K, width = block.shape
    T = width // 2
    count = tiles.shape[0]
    depth = stage.shape[0]

    def fetch(s, slot):
        return pltpu.make_async_copy(tiles.at[s], stage.at[slot], stage_sems.at[slot])

    for s in range(depth):
        fetch(s, s).start()
    greet(near_peers(place) + sum_peers(place))
    wires = Wires(place, send_sems, recv_sems)

    def split_tiles(start, stop, more):
        def step(s, carry):
            slot = lax.rem(s, depth)
            fetch(s, slot).wait()
            pairs[s, 0], pairs[s, 1] = split(stage[slot])
            if more:
                fetch(s + depth, slot).start()
            return carry

        lax.fori_loop(start, stop, step, 0)

    def prepare():
        for start in range(0, count, depth):
            split_tiles(start, start + depth, start + depth < count)
            yield

    def apply(number):
        near, far, part_rows, part_cols, slots, *boxes = sets[number]
        return Application(
            place, wires, table, pairs, sums, near, far, part_rows, part_cols, boxes, slots
        )

    sums[0] = jnp.zeros((K, T), F32)
    first = apply(0)

    def place_block():
        for u in range(2):
            half = block[:, u * T : (u + 1) * T]
            first.near[place.col * 2 + u] = half
            first.far[place.row * 2 + u] = half

    halves, total = first.run(
        lambda u: block.at[:, pl.ds(u * T, T)], place_block, prepare(), fold
    )
    mean = unfold(total) / total_rows
    for u in range(2):
        resid[u] = halves[u] - dot_n(mean, block[:, u * T : (u + 1) * T], HIGHEST)
    second = apply(1)
    local = {}

    def place_resid():
        grams[0] = mean
        cross = jnp.zeros((K, K), F32)
        square = jnp.zeros((K, K), F32)
        for u in range(2):
            image_x[:, u * T : (u + 1) * T] = halves[u]
            value = resid[u]
            second.near[place.col * 2 + u] = value
            second.far[place.row * 2 + u] = value
            cross += dot_t(halves[u], value, HIGHEST)
            square += dot_t(value, value, HIGHEST)
        grams[1] = cross
        grams[3] = square

    def make_small(middle):
        return jnp.concatenate([fold(grams[1]), fold(middle), fold(grams[3])], axis=0)

    halves, total = second.run(lambda u: resid.at[u], place_resid, (), make_small)
    for u in range(2):
        image_w[:, u * T : (u + 1) * T] = halves[u]
    half = K // 2
    for i in range(3):
        grams[1 + i] = unfold(total[i * half : (i + 1) * half]) / total_rows
    wires.drain()


def table_kernel(count, row_ids, col_ids, table):
    live = count[0]
    slots = row_ids.shape[0]

    def clear(s, carry):
        for line in range(2, 6):
            table[line, s] = 0
        return carry

    lax.fori_loop(0, slots, clear, 0)

    def step(s, carry):
        row, col = row_ids[s], col_ids[s]
        table[0, s] = row
        table[1, s] = col
        alive = s < live
        for line, at in ((4, row), (5, col)):
            before = table[line, at]
            table[line - 2, s] = jnp.where(alive, before, 0)
            table[line, at] = jnp.where(alive, s + 1, before)
        return carry

    lax.fori_loop(0, slots, step, 0)


def vmem(count):
    return [pl.BlockSpec(memory_space=pltpu.VMEM)] * count


def on_device(tile_count, tile_rows, tile_cols, tiles, block):
    K, width = block.shape
    T = tiles.shape[-1]
    slots = tiles.shape[2]
    total_rows = width * lax.axis_size("row") * lax.axis_size("col")
    smem = pl.BlockSpec(memory_space=pltpu.SMEM)
    table = pl.pallas_call(
        table_kernel,
        out_shape=jax.ShapeDtypeStruct((6, slots), jnp.int32),
        in_specs=[smem] * 3,
        out_specs=smem,
        name="slot_table",
    )(tile_count[0], tile_rows[0, 0], tile_cols[0, 0])
    strip = pltpu.VMEM((32, K, T), F32)
    seg = jax.ShapeDtypeStruct((K, width), F32)

    def one_set(rows):
        return [strip] * 4 + [pltpu.VMEM((5, 4, rows, 2 * K), F32)] + reduce_scratch(K, T)

    return pl.pallas_call(
        functools.partial(whole_kernel, total_rows),
        out_shape=(seg, seg, jax.ShapeDtypeStruct((4, K, K), F32)),
        in_specs=[smem, pl.BlockSpec(memory_space=pl.ANY)] + vmem(1),
        out_specs=tuple(vmem(3)),
        scratch_shapes=[
            pltpu.VMEM((8, T, T), F32),
            pltpu.SemaphoreType.DMA((8,)),
            pltpu.VMEM((slots, 2, T, T), BF16),
            pltpu.VMEM((slots + 1, K, T), F32),
            pltpu.VMEM((2, K, T), F32),
            pltpu.SemaphoreType.DMA((280,)),
            pltpu.SemaphoreType.DMA((280,)),
        ]
        + one_set(K // 2)
        + one_set(3 * K // 2),
        compiler_params=pltpu.CompilerParams(
            collective_id=0, has_side_effects=True, vmem_limit_bytes=VMEM_LIMIT
        ),
        name="rayleigh_ritz",
    )(table, tiles[0, 0], block)


def solution(mesh):
    return jax.shard_map(
        on_device,
        mesh=mesh,
        in_specs=(
            P("row", "col"),
            P("row", "col", None),
            P("row", "col", None),
            P("row", "col", None, None, None),
            P(None, ("row", "col")),
        ),
        out_specs=(P(None, ("row", "col")), P(None, ("row", "col")), P()),
        check_vma=False,
    )
```

```python
import functools

import jax
import jax.numpy as jnp
from jax import lax
from jax.experimental import pallas as pl
from jax.experimental.pallas import tpu as pltpu
from jax.sharding import PartitionSpec as P

MESH = pl.DeviceIdType.MESH
HIGHEST = lax.Precision.HIGHEST
F32 = jnp.float32
BF16 = jnp.bfloat16
RING = 4
VMEM_LIMIT = 60 * 1024 * 1024
UNROLL = 8
CHUNKS = 5
PREPARE = 4
STAGE = 16
(
    KSTART, KOWN, KZL, KZP, KZM, KZO, KXA, KXB, KYP, KYM, KYO, KNEAR, KFAR, KP, KU, KCOLS, KL,
    KROWS, KOP, KOM, KPP, KPM, KRL, KRH, KTA, KTB, KCO, KCI, KQO, KQM, KQP, KQN, KQL, KQH, KQA, KQB,
    KWO, KWQ, KWP, KWM, KWL, KWH, KE, KS, KT,
) = range(45)
(
    TO_XP, TO_XM, TO_YP, TO_YM, TO_CORE, TO_ZP, TO_ZM, TO_ZL, FZP, FZM, FXP, FXM, FYP, FYM,
) = range(14)
(
    DZ, DL, DX, DY,
) = range(4)
START = (
    (DZ, 0), (DL, 0), (DX, 0), (DY, 0), (DL, 1), (DZ, 1), (DX, 1), (DY, 1),
)
SUM_ORDER = (0, 4, 1, 3, 2)
EARLY_ORDER = (3, 1, 4, 2, 0)
FIRST_ORDER = (
    0, 31, 32, 33, 34, 9, 17, 18, 35, 36, 10, 2, 20, 21, 7, 1, 37, 19, 5, 38, 3, 39, 11, 22, 40, 6, 23, 24, 41,
    14, 8, 26, 27, 13, 4, 25, 12, 28, 29, 16, 42, 43, 44, 15, 45, 46, 47, 54, 55, 63, 70, 56, 57, 62, 71, 30,
    48, 119, 58, 74, 59, 67, 49, 64, 120, 73, 50, 51, 65, 72, 52, 66, 53, 86, 75, 60, 111, 61, 112, 87, 91, 80,
    99, 81, 92, 88, 93, 100, 89, 78, 101, 79, 121, 69, 113, 90, 94, 102, 76, 114, 103, 104, 95, 96, 68, 77, 122,
    115, 105, 116, 106, 107, 82, 83, 108, 97, 98, 123, 109, 84, 85, 110, 117, 124, 118,
)
SECOND_ORDER = (
    0, 31, 115, 9, 17, 18, 10, 20, 21, 2, 7, 1, 116, 19, 5, 3, 22, 11, 23, 24, 6, 26, 14, 8, 27, 13, 117, 4, 25,
    12, 28, 29, 32, 16, 33, 34, 15, 35, 36, 37, 44, 45, 53, 60, 118, 46, 47, 52, 61, 30, 38, 109, 48, 64, 49,
    57, 39, 54, 110, 63, 40, 41, 55, 62, 42, 56, 43, 76, 65, 119, 50, 101, 51, 102, 77, 81, 70, 89, 71, 82, 78,
    83, 90, 79, 68, 91, 69, 111, 59, 103, 80, 84, 92, 66, 104, 93, 120, 94, 85, 86, 58, 67, 112, 105, 95, 106,
    96, 97, 72, 73, 98, 87, 88, 113, 99, 74, 75, 100, 107, 114, 108,
)


class Place:
    def __init__(self):
        row = lax.axis_index("row")
        col = lax.axis_index("col")
        self.x, self.zh = lax.div(row, RING), lax.rem(row, RING)
        self.y = lax.div(col, RING)
        rest = lax.rem(col, RING)
        self.zl, self.core = lax.div(rest, 2), lax.rem(rest, 2)
        self.row, self.col = row, col

    def turn(self, value, by):
        return lax.rem(value + by, RING)

    def row_at(self, dx=0, dz=0):
        return self.turn(self.x, dx) * RING + self.turn(self.zh, dz)

    def col_at(self, dy=0, flip_zl=False, flip_core=False):
        zl = 1 - self.zl if flip_zl else self.zl
        core = 1 - self.core if flip_core else self.core
        return (self.turn(self.y, dy) * 2 + zl) * 2 + core

    def peer(self, dx=0, dz=0, dy=0, flip_zl=False, flip_core=False):
        return (self.row_at(dx, dz), self.col_at(dy, flip_zl, flip_core))


class Wires:
    def __init__(self, place, send_sems, recv_sems):
        self.place, self.send_sems, self.recv_sems = place, send_sems, recv_sems
        self.sent = []

    def send(self, src, dst, peer):
        number = len(self.sent)
        copy = pltpu.make_async_remote_copy(
            src_ref=src,
            dst_ref=dst,
            send_sem=self.send_sems.at[number],
            recv_sem=self.recv_sems.at[number],
            device_id=peer,
            device_id_type=MESH,
        )
        copy.start()
        self.sent.append(copy)
        return number

    def arrived(self, number, landing):
        pltpu.make_async_remote_copy(
            src_ref=landing,
            dst_ref=landing,
            send_sem=self.send_sems.at[number],
            recv_sem=self.recv_sems.at[number],
            device_id=self.place.peer(flip_core=True),
            device_id_type=MESH,
        ).wait_recv()

    def drain(self):
        for copy in self.sent:
            copy.wait_send()


def greet(peers):
    barrier = pltpu.get_barrier_semaphore()
    for peer in peers:
        pl.semaphore_signal(barrier, inc=1, device_id=peer, device_id_type=MESH)
    pl.semaphore_wait(barrier, len(peers))


def near_peers(place):
    return [
        place.peer(dx=1),
        place.peer(dx=3),
        place.peer(dz=1),
        place.peer(dz=3),
        place.peer(dy=1),
        place.peer(dy=3),
        place.peer(flip_zl=True),
        place.peer(flip_core=True),
    ]


def sum_peers(place):
    return [place.peer(dx=2), place.peer(dz=2), place.peer(dy=2)]


class Step:
    def __init__(self, before, waits, act):
        self.before, self.waits, self.act = before, waits, act

    def run(self, wires):
        for number, landing in self.waits():
            wires.arrived(number, landing)
        self.act()


def nothing():
    return ()


def gather_steps(place, wires, own, near, far, steps):
    send = wires.send

    def far_at(u, dx=0, dz=0):
        return far.at[place.row_at(dx, dz) * 2 + u]

    def near_at(u, dy=0, flip_zl=False, flip_core=False):
        return near.at[place.col_at(dy, flip_zl, flip_core) * 2 + u]

    xp, xm = place.peer(dx=1), place.peer(dx=3)
    zp, zm = place.peer(dz=1), place.peer(dz=3)
    yp, ym = place.peer(dy=1), place.peer(dy=3)
    zl_peer, core_peer = place.peer(flip_zl=True), place.peer(flip_core=True)
    sent = {}

    def x_out(dz, u, src):
        sent[TO_XP, dz, u] = send(src, far_at(u, dz=dz), xp)
        sent[TO_XM, dz, u] = send(src, far_at(u, dz=dz), xm)

    def y_out(flip, u, src):
        sent[TO_YP, flip, u] = send(src, near_at(u, flip_zl=flip), yp)
        sent[TO_YM, flip, u] = send(src, near_at(u, flip_zl=flip), ym)

    def share(dy, flip, u, src):
        sent[TO_CORE, dy, flip, u] = send(src, near_at(u, dy, flip), core_peer)

    def start():
        for name, u in START:
            if name == DZ:
                sent[TO_ZP, u] = send(own(u), far_at(u), zp)
                sent[TO_ZM, 1 - u] = send(own(1 - u), far_at(1 - u), zm)
            elif name == DL:
                sent[TO_ZL, u] = send(own(u), near_at(u), zl_peer)
            elif name == DX:
                x_out(0, u, own(u))
            else:
                y_out(False, u, own(u))
        for u in range(2):
            share(0, False, u, own(u))

    steps[(KSTART,)] = Step((), nothing, start)

    def add(name, key, landing, act, before=((KSTART,),)):
        steps[name] = Step(before, lambda: [(sent[key], landing)], act)

    for u in range(2):

        def zl_in(u=u):
            y_out(True, u, near_at(u, flip_zl=True))
            share(0, True, u, near_at(u, flip_zl=True))

        add((KZL, u), (TO_ZL, u), near_at(u, flip_zl=True), zl_in)

        def zp_in(u=u):
            if u == 0:
                sent[FZP] = send(far_at(0, dz=3), far_at(0, dz=3), zp)
            x_out(3, u, far_at(u, dz=3))

        def zm_in(u=u):
            if u == 1:
                sent[FZM] = send(far_at(1, dz=1), far_at(1, dz=1), zm)
            x_out(1, u, far_at(u, dz=1))

        add((KZP, u), (TO_ZP, u), far_at(u, dz=3), zp_in)
        add((KZM, u), (TO_ZM, u), far_at(u, dz=1), zm_in)
        key, before = (FZP, (KZP, 0)) if u == 0 else (FZM, (KZM, 1))
        add(
            (KZO, u),
            key,
            far_at(u, dz=2),
            lambda u=u: x_out(2, u, far_at(u, dz=2)),
            (before,),
        )
    origins = {
        0: ((KSTART,), (KSTART,)),
        3: ((KZP, 0), (KZP, 1)),
        1: ((KZM, 0), (KZM, 1)),
        2: ((KZO, 0), (KZO, 1)),
    }
    for dz in (0, 3, 1, 2):

        def plus_in(dz=dz):
            sent[FXP, dz] = send(far_at(0, dx=3, dz=dz), far_at(0, dx=3, dz=dz), xp)

        def minus_in(dz=dz):
            sent[FXM, dz] = send(far_at(1, dx=1, dz=dz), far_at(1, dx=1, dz=dz), xm)

        add((KXA, dz), (TO_XP, dz, 0), far_at(0, dx=3, dz=dz), plus_in, (origins[dz][0],))
        add((KXB, dz), (TO_XM, dz, 1), far_at(1, dx=1, dz=dz), minus_in, (origins[dz][1],))
    for flip in (False, True):
        for u in range(2):
            before = ((KZL, u),) if flip else ((KSTART,),)

            def plus_y(flip=flip, u=u):
                if u == 0:
                    sent[FYP, flip] = send(near_at(0, 3, flip), near_at(0, 3, flip), yp)
                share(3, flip, u, near_at(u, 3, flip))

            def minus_y(flip=flip, u=u):
                if u == 1:
                    sent[FYM, flip] = send(near_at(1, 1, flip), near_at(1, 1, flip), ym)
                share(1, flip, u, near_at(u, 1, flip))

            add((KYP, int(flip), u), (TO_YP, flip, u), near_at(u, 3, flip), plus_y, before)
            add((KYM, int(flip), u), (TO_YM, flip, u), near_at(u, 1, flip), minus_y, before)
            key, origin = (FYP, KYP) if u == 0 else (FYM, KYM)
            add(
                (KYO, int(flip), u),
                (key, flip),
                near_at(u, 2, flip),
                lambda flip=flip, u=u: share(2, flip, u, near_at(u, 2, flip)),
                ((origin, int(flip), u),),
            )

    def near_waits():
        return [
            (sent[TO_CORE, dy, flip, u], near_at(u, dy, flip, True))
            for flip in (False, True)
            for dy in (0, 1, 3, 2)
            for u in range(2)
        ]

    def far_waits():
        waits = []
        for dz in (0, 3, 1, 2):
            waits.append((sent[TO_XM, dz, 0], far_at(0, dx=1, dz=dz)))
            waits.append((sent[TO_XP, dz, 1], far_at(1, dx=3, dz=dz)))
            waits.append((sent[FXP, dz], far_at(0, dx=2, dz=dz)))
            waits.append((sent[FXM, dz], far_at(1, dx=2, dz=dz)))
        return waits

    y_names = tuple(n for n in steps if n[0] in (KZL, KYP, KYM, KYO))
    x_names = tuple(n for n in steps if n[0] in (KZP, KZM, KZO, KXA, KXB))
    steps[(KNEAR,)] = Step(((KOWN,),) + y_names, near_waits, lambda: None)
    steps[(KFAR,)] = Step(((KOWN,),) + x_names, far_waits, lambda: None)


class RingSum:
    def __init__(self, wires, term, box, pair, plus, minus):
        self.wires, self.term, self.box, self.pair = wires, term, box, pair
        self.plus, self.minus = plus, minus

    def opposite_plus(self):
        self.opp_plus = self.wires.send(self.term(2, 0), self.box(0), self.plus)

    def opposite_minus(self):
        self.opp_minus = self.wires.send(self.term(2, 1), self.box(1), self.minus)

    def plain_plus(self):
        self.plus_sent = self.wires.send(self.term(1, 1), self.box(2), self.plus)

    def plain_minus(self):
        self.minus_sent = self.wires.send(self.term(3, 0), self.box(3), self.minus)

    def low_waits(self):
        return [(self.opp_plus, self.box(0))]

    def join_low(self):
        self.pair(0)[...] = self.term(1, 0)[...] + self.box(0)[...]
        self.low_sent = self.wires.send(self.pair(0), self.box(4), self.plus)

    def high_waits(self):
        return [(self.opp_minus, self.box(1))]

    def join_high(self):
        self.pair(1)[...] = self.term(3, 1)[...] + self.box(1)[...]
        self.high_sent = self.wires.send(self.pair(1), self.box(5), self.minus)

    def low_total_waits(self):
        return [(self.minus_sent, self.box(3)), (self.low_sent, self.box(4))]

    def high_total_waits(self):
        return [(self.plus_sent, self.box(2)), (self.high_sent, self.box(5))]

    def low_total(self):
        return self.term(0, 0)[...] + (self.box(4)[...] + self.box(3)[...])

    def high_total(self):
        return self.term(0, 1)[...] + (self.box(2)[...] + self.box(5)[...])


class SmallSum:
    def __init__(self, place, wires, slots):
        self.place, self.wires, self.slots = place, wires, slots

    def pair_out(self, stage, value, mine, peer):
        self.mine = mine
        self.slots[stage, mine] = value
        self.numbers = [self.wires.send(self.slots.at[stage, mine], self.slots.at[stage, mine], peer)]

    def pair_waits(self, stage):
        return [(self.numbers[0], self.slots.at[stage, 1 - self.mine])]

    def pair_in(self, stage):
        return self.slots[stage, 0] + self.slots[stage, 1]

    def ring_out(self, stage, value, mine, peers):
        self.mine = mine
        self.slots[stage, mine] = value
        self.numbers = [
            self.wires.send(self.slots.at[stage, mine], self.slots.at[stage, mine], peers[by])
            for by in (1, 2, 3)
        ]

    def ring_waits(self, stage):
        return [
            (number, self.slots.at[stage, lax.rem(self.mine + RING - by, RING)])
            for number, by in zip(self.numbers, (1, 2, 3))
        ]

    def ring_in(self, stage):
        return (self.slots[stage, 0] + self.slots[stage, 1]) + (self.slots[stage, 2] + self.slots[stage, 3])

    def add_steps(self, steps, kind, order, make_value, before):
        place = self.place
        places = (place.core, place.zl, place.y, place.x, place.zh)

        def out(stage, value):
            axis = order[stage]
            if axis == 0:
                self.pair_out(stage, value, places[axis], place.peer(flip_core=True))
            elif axis == 1:
                self.pair_out(stage, value, places[axis], place.peer(flip_zl=True))
            elif axis == 2:
                self.ring_out(stage, value, places[axis], {by: place.peer(dy=by) for by in (1, 2, 3)})
            elif axis == 3:
                self.ring_out(stage, value, places[axis], {by: place.peer(dx=by) for by in (1, 2, 3)})
            else:
                self.ring_out(stage, value, places[axis], {by: place.peer(dz=by) for by in (1, 2, 3)})

        def waits(stage):
            return self.pair_waits(stage) if order[stage] < 2 else self.ring_waits(stage)

        def take(stage):
            return self.pair_in(stage) if order[stage] < 2 else self.ring_in(stage)

        def last():
            self.result = take(4)

        steps[(kind, 0)] = Step(before, nothing, lambda: out(0, make_value()))
        for stage in range(1, 5):
            steps[(kind, stage)] = Step(
                ((kind, stage - 1),),
                functools.partial(waits, stage - 1),
                lambda stage=stage: out(stage, take(stage - 1)),
            )
        steps[(kind, 5)] = Step(((kind, 4),), functools.partial(waits, 4), last)


class Reduction:
    depths = (2, 1, 3, 0)

    def __init__(self, place, wires, part_rows, part_cols, boxes):
        self.place, self.wires = place, wires
        self.part_rows = part_rows
        (
            self.core_box,
            self.near_sum,
            y_box,
            y_pair,
            self.y_held,
            self.zl_box,
            x_box,
            x_pair,
            self.x_held,
            z_box,
            z_pair,
        ) = boxes
        xp, xm = place.peer(dx=1), place.peer(dx=3)
        zp, zm = place.peer(dz=1), place.peer(dz=3)
        yp, ym = place.peer(dy=1), place.peer(dy=3)
        self.zl_peer = place.peer(flip_zl=True)
        self.core_peer = place.peer(flip_core=True)

        def x_ring(k, dz):
            return RingSum(
                wires,
                lambda d, u: part_cols.at[place.row_at(d, dz) * 2 + u],
                lambda i: x_box.at[k, i],
                lambda i: x_pair.at[k, i],
                xp,
                xm,
            )

        def y_ring(flip):
            return RingSum(
                wires,
                lambda d, u: self.near_sum.at[d, int(flip), u],
                lambda i: y_box.at[int(flip), i],
                lambda i: y_pair.at[int(flip), i],
                yp,
                ym,
            )

        self.x = [x_ring(k, dz) for k, dz in enumerate(self.depths)]
        self.y = {flip: y_ring(flip) for flip in (True, False)}
        self.z = RingSum(
            wires,
            lambda d, u: self.x_held.at[self.depths.index(d), u],
            lambda i: z_box.at[i],
            lambda i: z_pair.at[i],
            zp,
            zm,
        )

    def cross_out(self):
        self.crossed = {}
        for dy in (2, 1, 3, 0):
            for flip in (True, False):
                source = self.place.col_at(dy, flip, True) * 2
                self.crossed[dy, flip] = self.wires.send(
                    self.part_rows.at[pl.ds(source, 2)],
                    self.core_box.at[dy, int(flip)],
                    self.core_peer,
                )

    def cross_waits(self, dy, flip):
        return [(self.crossed[dy, flip], self.core_box.at[dy, int(flip)])]

    def cross_in(self, dy, flip):
        source = self.place.col_at(dy, flip) * 2
        self.near_sum[dy, int(flip)] = self.part_rows[pl.ds(source, 2)] + self.core_box[dy, int(flip)]

    def low_x(self, k):
        self.x_held[k, 0] = self.x[k].low_total()

    def high_x(self, k):
        self.x_held[k, 1] = self.x[k].high_total()

    def low_y(self, flip):
        self.y_held[int(flip), 0] = self.y[flip].low_total()
        self.zl_share(flip, 0)

    def high_y(self, flip):
        self.y_held[int(flip), 1] = self.y[flip].high_total()
        self.zl_share(flip, 1)

    def zl_share(self, flip, u):
        if flip:
            self.zl_sent[u] = self.wires.send(self.y_held.at[1, u], self.zl_box.at[u], self.zl_peer)

    def finish(self, u):
        total = self.z.high_total() if u else self.z.low_total()
        self.result[u] = total + (self.y_held[0, u] + self.zl_box[u])

    def add_steps(self, steps):
        self.zl_sent, self.result = {}, {}
        for k, ring in enumerate(self.x):
            steps[(KOP, k)] = Step(((KCOLS,),), nothing, ring.opposite_plus)
            steps[(KOM, k)] = Step(((KCOLS,),), nothing, ring.opposite_minus)
            steps[(KPP, k)] = Step(((KCOLS,),), nothing, ring.plain_plus)
            steps[(KPM, k)] = Step(((KCOLS,),), nothing, ring.plain_minus)
            steps[(KRL, k)] = Step(((KOP, k),), ring.low_waits, ring.join_low)
            steps[(KRH, k)] = Step(((KOM, k),), ring.high_waits, ring.join_high)
            steps[(KTA, k)] = Step(
                ((KRL, k), (KPM, k)), ring.low_total_waits, functools.partial(self.low_x, k)
            )
            steps[(KTB, k)] = Step(
                ((KRH, k), (KPP, k)), ring.high_total_waits, functools.partial(self.high_x, k)
            )
        steps[(KCO,)] = Step(((KROWS,),), nothing, self.cross_out)
        for flip in (True, False):
            f = int(flip)
            ring = self.y[flip]
            for dy in (2, 1, 3, 0):
                steps[(KCI, dy, f)] = Step(
                    ((KCO,),),
                    functools.partial(self.cross_waits, dy, flip),
                    functools.partial(self.cross_in, dy, flip),
                )
            steps[(KQO, f)] = Step(((KCI, 2, f),), nothing, ring.opposite_plus)
            steps[(KQM, f)] = Step(((KCI, 2, f),), nothing, ring.opposite_minus)
            steps[(KQP, f)] = Step(((KCI, 1, f),), nothing, ring.plain_plus)
            steps[(KQN, f)] = Step(((KCI, 3, f),), nothing, ring.plain_minus)
            steps[(KQL, f)] = Step(((KQO, f), (KCI, 1, f)), ring.low_waits, ring.join_low)
            steps[(KQH, f)] = Step(((KQM, f), (KCI, 3, f)), ring.high_waits, ring.join_high)
            steps[(KQA, f)] = Step(
                ((KQL, f), (KQN, f), (KCI, 0, f)),
                ring.low_total_waits,
                functools.partial(self.low_y, flip),
            )
            steps[(KQB, f)] = Step(
                ((KQH, f), (KQP, f), (KCI, 0, f)),
                ring.high_total_waits,
                functools.partial(self.high_y, flip),
            )
        steps[(KWO,)] = Step(((KTA, 0),), nothing, self.z.opposite_plus)
        steps[(KWQ,)] = Step(((KTB, 0),), nothing, self.z.opposite_minus)
        steps[(KWP,)] = Step(((KTB, 1),), nothing, self.z.plain_plus)
        steps[(KWM,)] = Step(((KTA, 2),), nothing, self.z.plain_minus)
        steps[(KWL,)] = Step(((KWO,), (KTA, 1)), self.z.low_waits, self.z.join_low)
        steps[(KWH,)] = Step(((KWQ,), (KTB, 2)), self.z.high_waits, self.z.join_high)
        steps[(KE, 0)] = Step(
            ((KWM,), (KWL,), (KTA, 3), (KQA, 0), (KQA, 1)),
            lambda: [(self.zl_sent[0], self.zl_box.at[0])] + self.z.low_total_waits(),
            lambda: self.finish(0),
        )
        steps[(KE, 1)] = Step(
            ((KWP,), (KWH,), (KTB, 3), (KQB, 0), (KQB, 1)),
            lambda: [(self.zl_sent[1], self.zl_box.at[1])] + self.z.high_total_waits(),
            lambda: self.finish(1),
        )


def reduce_scratch(K, T):
    return [
        pltpu.VMEM((4, 2, 2, K, T), F32),
        pltpu.VMEM((4, 2, 2, K, T), F32),
        pltpu.VMEM((2, 6, K, T), F32),
        pltpu.VMEM((2, 2, K, T), F32),
        pltpu.VMEM((2, 2, K, T), F32),
        pltpu.VMEM((2, K, T), F32),
        pltpu.VMEM((4, 6, K, T), F32),
        pltpu.VMEM((4, 2, K, T), F32),
        pltpu.VMEM((4, 2, K, T), F32),
        pltpu.VMEM((6, K, T), F32),
        pltpu.VMEM((2, K, T), F32),
    ]


def split(value):
    high = value.astype(BF16)
    low = (value - high.astype(F32)).astype(BF16)
    return high, low


def dot_t(left, right, precision=None):
    return lax.dot_general(
        left, right, (((1,), (1,)), ((), ())), precision=precision, preferred_element_type=F32
    )


def dot_n(left, right, precision=None):
    return lax.dot_general(
        left, right, (((1,), (0,)), ((), ())), precision=precision, preferred_element_type=F32
    )


def fold(square):
    half = square.shape[0] // 2
    return jnp.concatenate([square[:half], square[half:]], axis=1)


def unfold(flat):
    half = flat.shape[1] // 2
    return jnp.concatenate([flat[:, :half], flat[:, half:]], axis=0)


def energy(part, vectors):
    K = part.shape[1]
    group = 4

    def step(g, total):
        left = [jnp.concatenate(split(part[g * group + i]), axis=0) for i in range(group)]
        right = [jnp.concatenate(split(vectors[g * group + i]), axis=0) for i in range(group)]
        return total + dot_t(jnp.concatenate(left, axis=1), jnp.concatenate(right, axis=1))

    total = lax.fori_loop(0, part.shape[0] // group, step, jnp.zeros((2 * K, 2 * K), F32))
    total = total[:K] + total[K:]
    total = total[:, :K] + total[:, K:]
    return total + total.T


class Application:
    def __init__(
        self, place, wires, table, pairs, sums, near, far, part_rows, part_cols, boxes, slots, early_slots
    ):
        self.place, self.wires, self.table, self.pairs, self.sums = place, wires, table, pairs, sums
        self.near, self.far = near, far
        self.part_rows, self.part_cols = part_rows, part_cols
        self.slots, self.early_slots = slots, early_slots
        self.reduction = Reduction(place, wires, part_rows, part_cols, boxes)

    def products(self, vectors, ids, before, transposed, start, stop):
        K = self.near.shape[1]
        dot = dot_t if transposed else dot_n

        def product(s):
            high, low = split(vectors[self.table[ids, s]])
            both = dot(jnp.concatenate([high, low], axis=0), self.pairs[s, 0])
            return (both[:K] + both[K:]) + dot(high, self.pairs[s, 1])

        def step(group, carry):
            slots = [group * UNROLL + i for i in range(UNROLL)]
            for s, value in zip(slots, [product(s) for s in slots]):
                self.sums[s + 1] = value + self.sums[self.table[before, s]]
            return carry

        lax.fori_loop(start // UNROLL, stop // UNROLL, step, 0)

    def upper(self, start, stop):
        self.products(self.near, 0, 3, False, start, stop)

    def lower(self, start, stop):
        self.products(self.far, 1, 2, True, start, stop)

    def collect(self, line, parts):
        def step(group, carry):
            for i in range(4):
                p = group * 4 + i
                parts[p] = self.sums[self.table[line, p]]
            return carry

        lax.fori_loop(0, parts.shape[0] // 4, step, 0)

    def steps(self, own, place_own, prepare, early):
        steps = {}
        gather_steps(self.place, self.wires, own, self.near, self.far, steps)
        steps[(KOWN,)] = Step(((KSTART,),), nothing, place_own)
        ready = ()
        for i, chunk in enumerate(prepare):
            steps[(KP, i)] = Step(ready, nothing, chunk)
            ready = ((KP, i),)
        last = ((KNEAR,),) + ready
        for i in range(CHUNKS):
            size = self.pairs.shape[0] // CHUNKS
            act = functools.partial(self.upper, i * size, (i + 1) * size)
            steps[(KU, i)] = Step(last, nothing, act)
            last = ((KU, i),)
        steps[(KCOLS,)] = Step(last, nothing, lambda: self.collect(5, self.part_cols))
        last = ((KFAR,), (KCOLS,))
        for i in range(CHUNKS):
            act = functools.partial(self.lower, i * size, (i + 1) * size)
            steps[(KL, i)] = Step(last, nothing, act)
            last = ((KL, i),)
        steps[(KROWS,)] = Step(last, nothing, lambda: self.collect(4, self.part_rows))
        self.reduction.add_steps(steps)
        self.small = SmallSum(self.place, self.wires, self.slots)
        self.early = SmallSum(self.place, self.wires, self.early_slots)
        self.small.add_steps(
            steps,
            KS,
            SUM_ORDER,
            lambda: fold(energy(self.part_cols, self.far)),
            ((KFAR,), (KCOLS,)),
        )
        if early is not None:
            self.early.add_steps(steps, KT, EARLY_ORDER, early, ((KOWN,),))
        return steps

    def run(self, order, own, place_own, prepare, early):
        steps = self.steps(own, place_own, prepare, early)
        names = list(steps)
        done = set()
        for number in order:
            name = names[number]
            assert set(steps[name].before) <= done and name not in done, name
            steps[name].run(self.wires)
            done.add(name)
        assert len(done) == len(steps)
        return self.reduction.result, self.small.result


def whole_kernel(total_rows, table, tiles, block, image_x, image_w, grams, *scratch):
    (stage, stage_sems, pairs, sums, resid, early_slots, send_sems, recv_sems), scratch = (
        scratch[:8],
        scratch[8:],
    )
    sets = scratch[: len(scratch) // 2], scratch[len(scratch) // 2 :]
    place = Place()
    K, width = block.shape
    T = width // 2
    count = tiles.shape[0]
    depth = stage.shape[0]

    def fetch(s, slot):
        return pltpu.make_async_copy(tiles.at[s], stage.at[slot], stage_sems.at[slot])

    for s in range(depth):
        fetch(s, s).start()
    greet(near_peers(place) + sum_peers(place))
    wires = Wires(place, send_sems, recv_sems)

    def split_tiles(start, stop, more):
        def step(s, carry):
            slot = lax.rem(s, depth)
            fetch(s, slot).wait()
            pairs[s, 0], pairs[s, 1] = split(stage[slot])
            if more:
                fetch(s + depth, slot).start()
            return carry

        lax.fori_loop(start, stop, step, 0)

    prepare = [
        functools.partial(split_tiles, start, start + PREPARE, start + PREPARE + depth <= count)
        for start in range(0, count, PREPARE)
    ]

    def apply(number):
        near, far, part_rows, part_cols, slots, *boxes = sets[number]
        return Application(
            place, wires, table, pairs, sums, near, far, part_rows, part_cols, boxes, slots, early_slots
        )

    sums[0] = jnp.zeros((K, T), F32)
    first = apply(0)

    def place_block():
        for u in range(2):
            half = block[:, u * T : (u + 1) * T]
            first.near[place.col * 2 + u] = half
            first.far[place.row * 2 + u] = half

    halves, total = first.run(
        FIRST_ORDER,
        lambda u: block.at[:, pl.ds(u * T, T)], place_block, prepare, None
    )
    mean = unfold(total) / total_rows
    for u in range(2):
        resid[u] = halves[u] - dot_n(mean, block[:, u * T : (u + 1) * T], HIGHEST)
    second = apply(1)
    local = {}

    def place_resid():
        grams[0] = mean
        cross = jnp.zeros((K, K), F32)
        square = jnp.zeros((K, K), F32)
        for u in range(2):
            image_x[:, u * T : (u + 1) * T] = halves[u]
            value = resid[u]
            second.near[place.col * 2 + u] = value
            second.far[place.row * 2 + u] = value
            cross += dot_t(halves[u], value, HIGHEST)
            square += dot_t(value, value, HIGHEST)
        grams[1] = cross
        grams[3] = square

    def early():
        return jnp.concatenate([fold(grams[1]), fold(grams[3])], axis=0)

    halves, total = second.run(
        SECOND_ORDER, lambda u: resid.at[u], place_resid, (), early
    )
    for u in range(2):
        image_w[:, u * T : (u + 1) * T] = halves[u]
    half = K // 2
    grams[1] = unfold(second.early.result[:half]) / total_rows
    grams[2] = unfold(total) / total_rows
    grams[3] = unfold(second.early.result[half:]) / total_rows
    wires.drain()


def table_kernel(count, row_ids, col_ids, table):
    live = count[0]
    slots = row_ids.shape[0]

    def clear(s, carry):
        for line in range(2, 6):
            table[line, s] = 0
        return carry

    lax.fori_loop(0, slots, clear, 0)

    def step(s, carry):
        row, col = row_ids[s], col_ids[s]
        table[0, s] = row
        table[1, s] = col
        alive = s < live
        for line, at in ((4, row), (5, col)):
            before = table[line, at]
            table[line - 2, s] = jnp.where(alive, before, 0)
            table[line, at] = jnp.where(alive, s + 1, before)
        return carry

    lax.fori_loop(0, slots, step, 0)


def hand_over(*refs):
    half = len(refs) // 2
    for source, target in zip(refs[:half], refs[half:]):
        target[...] = source[...]


def vmem(count):
    return [pl.BlockSpec(memory_space=pltpu.VMEM)] * count


def on_device(tile_count, tile_rows, tile_cols, tiles, block):
    K, width = block.shape
    T = tiles.shape[-1]
    slots = tiles.shape[2]
    total_rows = width * lax.axis_size("row") * lax.axis_size("col")
    smem = pl.BlockSpec(memory_space=pltpu.SMEM)
    table = pl.pallas_call(
        table_kernel,
        out_shape=jax.ShapeDtypeStruct((6, slots), jnp.int32),
        in_specs=[smem] * 3,
        out_specs=smem,
        name="slot_table",
    )(tile_count[0], tile_rows[0, 0], tile_cols[0, 0])
    strip = pltpu.VMEM((32, K, T), F32)
    seg = jax.ShapeDtypeStruct((K, width), F32)

    one_set = [strip] * 4 + [pltpu.VMEM((5, 4, K // 2, 2 * K), F32)] + reduce_scratch(K, T)

    shapes = (seg, seg, jax.ShapeDtypeStruct((4, K, K), F32))
    results = pl.pallas_call(
        functools.partial(whole_kernel, total_rows),
        out_shape=shapes,
        in_specs=[smem, pl.BlockSpec(memory_space=pl.ANY)] + vmem(1),
        out_specs=tuple(vmem(3)),
        scratch_shapes=[
            pltpu.VMEM((STAGE, T, T), F32),
            pltpu.SemaphoreType.DMA((STAGE,)),
            pltpu.VMEM((slots, 2, T, T), BF16),
            pltpu.VMEM((slots + 1, K, T), F32),
            pltpu.VMEM((2, K, T), F32),
            pltpu.VMEM((5, 4, K, 2 * K), F32),
            pltpu.SemaphoreType.DMA((300,)),
            pltpu.SemaphoreType.DMA((300,)),
        ]
        + one_set * 2,
        compiler_params=pltpu.CompilerParams(
            collective_id=0, has_side_effects=True, vmem_limit_bytes=VMEM_LIMIT
        ),
        name="rayleigh_ritz",
    )(table, tiles[0, 0], block)
    return pl.pallas_call(
        hand_over,
        out_shape=shapes,
        in_specs=vmem(3),
        out_specs=tuple(vmem(3)),
        name="hand_over",
    )(*results)


def solution(mesh):
    return jax.shard_map(
        on_device,
        mesh=mesh,
        in_specs=(
            P("row", "col"),
            P("row", "col", None),
            P("row", "col", None),
            P("row", "col", None, None, None),
            P(None, ("row", "col")),
        ),
        out_specs=(P(None, ("row", "col")), P(None, ("row", "col")), P()),
        check_vma=False,
    )
```

```python
import functools

import jax
import jax.numpy as jnp
from jax import lax
from jax.experimental import pallas as pl
from jax.experimental.pallas import tpu as pltpu
from jax.sharding import PartitionSpec as P

MESH = pl.DeviceIdType.MESH
HIGHEST = lax.Precision.HIGHEST
F32 = jnp.float32
BF16 = jnp.bfloat16
RING = 4
VMEM_LIMIT = 60 * 1024 * 1024
UNROLL = 8
CHUNKS = 5
PREPARE = 2
STAGE = 16
(
    KSTART, KOWN, KZL, KZP, KZM, KZO, KXA, KXB, KYP, KYM, KYO, KNEAR, KFAR, KP, KU, KCOLS, KL,
    KROWS, KOP, KOM, KPP, KPM, KRL, KRH, KTA, KTB, KCO, KCI, KQO, KQM, KQP, KQN, KQL, KQH, KQA, KQB,
    KWO, KWQ, KWP, KWM, KWL, KWH, KE, KS, KT,
) = range(45)
(
    TO_XP, TO_XM, TO_YP, TO_YM, TO_CORE, TO_ZP, TO_ZM, TO_ZL, FZP, FZM, FXP, FXM, FYP, FYM,
) = range(14)
(
    DZ, DL, DX, DY,
) = range(4)
START = (
    (DZ, 0), (DL, 0), (DX, 0), (DY, 0), (DL, 1), (DZ, 1), (DX, 1), (DY, 1),
)
SUM_ORDER = (0, 4, 1, 3, 2)
EARLY_ORDER = (3, 1, 4, 2, 0)
FIRST_ORDER = (
    0, 31, 32, 33, 34, 35, 36, 37, 9, 17, 18, 38, 39, 40, 10, 20, 21, 2, 7, 41, 1, 42, 43, 5, 19, 44, 3, 45, 46,
    22, 11, 47, 48, 23, 24, 49, 6, 50, 8, 14, 26, 27, 13, 51, 4, 25, 12, 28, 16, 29, 52, 53, 54, 15, 55, 56, 57,
    64, 65, 73, 80, 66, 67, 72, 81, 30, 58, 129, 68, 69, 77, 84, 59, 74, 83, 130, 60, 61, 75, 82, 62, 63, 96,
    76, 85, 70, 121, 71, 122, 97, 101, 109, 88, 89, 102, 98, 103, 110, 99, 111, 90, 91, 131, 100, 79, 123, 112,
    104, 86, 124, 113, 114, 105, 106, 78, 87, 132, 125, 115, 126, 116, 92, 93, 117, 118, 107, 133, 108, 94, 95,
    119, 120, 127, 134, 128,
)
SECOND_ORDER = (
    0, 31, 115, 9, 17, 18, 10, 20, 21, 2, 7, 1, 116, 5, 19, 3, 22, 11, 23, 24, 6, 26, 14, 8, 27, 13, 117, 4, 25,
    12, 28, 29, 32, 16, 33, 34, 15, 35, 36, 37, 44, 45, 53, 60, 118, 46, 47, 52, 61, 30, 38, 109, 48, 49, 57,
    64, 39, 54, 63, 110, 40, 41, 55, 62, 42, 43, 76, 56, 65, 119, 50, 101, 51, 102, 77, 81, 89, 68, 69, 82, 78,
    83, 90, 79, 91, 70, 71, 111, 80, 59, 103, 92, 120, 84, 66, 104, 93, 94, 85, 86, 58, 67, 112, 105, 95, 106,
    96, 72, 73, 97, 98, 87, 113, 88, 74, 75, 99, 100, 107, 114, 108,
)


class Place:
    def __init__(self):
        row = lax.axis_index("row")
        col = lax.axis_index("col")
        self.x, self.zh = lax.div(row, RING), lax.rem(row, RING)
        self.y = lax.div(col, RING)
        rest = lax.rem(col, RING)
        self.zl, self.core = lax.div(rest, 2), lax.rem(rest, 2)
        self.row, self.col = row, col

    def turn(self, value, by):
        return lax.rem(value + by, RING)

    def row_at(self, dx=0, dz=0):
        return self.turn(self.x, dx) * RING + self.turn(self.zh, dz)

    def col_at(self, dy=0, flip_zl=False, flip_core=False):
        zl = 1 - self.zl if flip_zl else self.zl
        core = 1 - self.core if flip_core else self.core
        return (self.turn(self.y, dy) * 2 + zl) * 2 + core

    def peer(self, dx=0, dz=0, dy=0, flip_zl=False, flip_core=False):
        return (self.row_at(dx, dz), self.col_at(dy, flip_zl, flip_core))


class Wires:
    def __init__(self, place, send_sems, recv_sems):
        self.place, self.send_sems, self.recv_sems = place, send_sems, recv_sems
        self.sent = []

    def send(self, src, dst, peer):
        number = len(self.sent)
        copy = pltpu.make_async_remote_copy(
            src_ref=src,
            dst_ref=dst,
            send_sem=self.send_sems.at[number],
            recv_sem=self.recv_sems.at[number],
            device_id=peer,
            device_id_type=MESH,
        )
        copy.start()
        self.sent.append(copy)
        return number

    def arrived(self, number, landing):
        pltpu.make_async_remote_copy(
            src_ref=landing,
            dst_ref=landing,
            send_sem=self.send_sems.at[number],
            recv_sem=self.recv_sems.at[number],
            device_id=self.place.peer(flip_core=True),
            device_id_type=MESH,
        ).wait_recv()

    def drain(self):
        for copy in self.sent:
            copy.wait_send()


def greet(peers):
    barrier = pltpu.get_barrier_semaphore()
    for peer in peers:
        pl.semaphore_signal(barrier, inc=1, device_id=peer, device_id_type=MESH)
    pl.semaphore_wait(barrier, len(peers))


def near_peers(place):
    return [
        place.peer(dx=1),
        place.peer(dx=3),
        place.peer(dz=1),
        place.peer(dz=3),
        place.peer(dy=1),
        place.peer(dy=3),
        place.peer(flip_zl=True),
        place.peer(flip_core=True),
    ]


def sum_peers(place):
    return [place.peer(dx=2), place.peer(dz=2), place.peer(dy=2)]


class Step:
    def __init__(self, before, waits, act):
        self.before, self.waits, self.act = before, waits, act

    def run(self, wires):
        for number, landing in self.waits():
            wires.arrived(number, landing)
        self.act()


def nothing():
    return ()


def gather_steps(place, wires, own, near, far, steps):
    send = wires.send

    def far_at(u, dx=0, dz=0):
        return far.at[place.row_at(dx, dz) * 2 + u]

    def near_at(u, dy=0, flip_zl=False, flip_core=False):
        return near.at[place.col_at(dy, flip_zl, flip_core) * 2 + u]

    xp, xm = place.peer(dx=1), place.peer(dx=3)
    zp, zm = place.peer(dz=1), place.peer(dz=3)
    yp, ym = place.peer(dy=1), place.peer(dy=3)
    zl_peer, core_peer = place.peer(flip_zl=True), place.peer(flip_core=True)
    sent = {}

    def x_out(dz, u, src):
        sent[TO_XP, dz, u] = send(src, far_at(u, dz=dz), xp)
        sent[TO_XM, dz, u] = send(src, far_at(u, dz=dz), xm)

    def y_out(flip, u, src):
        sent[TO_YP, flip, u] = send(src, near_at(u, flip_zl=flip), yp)
        sent[TO_YM, flip, u] = send(src, near_at(u, flip_zl=flip), ym)

    def share(dy, flip, u, src):
        sent[TO_CORE, dy, flip, u] = send(src, near_at(u, dy, flip), core_peer)

    def start():
        for name, u in START:
            if name == DZ:
                sent[TO_ZP, u] = send(own(u), far_at(u), zp)
                sent[TO_ZM, 1 - u] = send(own(1 - u), far_at(1 - u), zm)
            elif name == DL:
                sent[TO_ZL, u] = send(own(u), near_at(u), zl_peer)
            elif name == DX:
                x_out(0, u, own(u))
            else:
                y_out(False, u, own(u))
        for u in range(2):
            share(0, False, u, own(u))

    steps[(KSTART,)] = Step((), nothing, start)

    def add(name, key, landing, act, before=((KSTART,),)):
        steps[name] = Step(before, lambda: [(sent[key], landing)], act)

    for u in range(2):

        def zl_in(u=u):
            y_out(True, u, near_at(u, flip_zl=True))
            share(0, True, u, near_at(u, flip_zl=True))

        add((KZL, u), (TO_ZL, u), near_at(u, flip_zl=True), zl_in)

        def zp_in(u=u):
            if u == 0:
                sent[FZP] = send(far_at(0, dz=3), far_at(0, dz=3), zp)
            x_out(3, u, far_at(u, dz=3))

        def zm_in(u=u):
            if u == 1:
                sent[FZM] = send(far_at(1, dz=1), far_at(1, dz=1), zm)
            x_out(1, u, far_at(u, dz=1))

        add((KZP, u), (TO_ZP, u), far_at(u, dz=3), zp_in)
        add((KZM, u), (TO_ZM, u), far_at(u, dz=1), zm_in)
        key, before = (FZP, (KZP, 0)) if u == 0 else (FZM, (KZM, 1))
        add(
            (KZO, u),
            key,
            far_at(u, dz=2),
            lambda u=u: x_out(2, u, far_at(u, dz=2)),
            (before,),
        )
    origins = {
        0: ((KSTART,), (KSTART,)),
        3: ((KZP, 0), (KZP, 1)),
        1: ((KZM, 0), (KZM, 1)),
        2: ((KZO, 0), (KZO, 1)),
    }
    for dz in (0, 3, 1, 2):

        def plus_in(dz=dz):
            sent[FXP, dz] = send(far_at(0, dx=3, dz=dz), far_at(0, dx=3, dz=dz), xp)

        def minus_in(dz=dz):
            sent[FXM, dz] = send(far_at(1, dx=1, dz=dz), far_at(1, dx=1, dz=dz), xm)

        add((KXA, dz), (TO_XP, dz, 0), far_at(0, dx=3, dz=dz), plus_in, (origins[dz][0],))
        add((KXB, dz), (TO_XM, dz, 1), far_at(1, dx=1, dz=dz), minus_in, (origins[dz][1],))
    for flip in (False, True):
        for u in range(2):
            before = ((KZL, u),) if flip else ((KSTART,),)

            def plus_y(flip=flip, u=u):
                if u == 0:
                    sent[FYP, flip] = send(near_at(0, 3, flip), near_at(0, 3, flip), yp)
                share(3, flip, u, near_at(u, 3, flip))

            def minus_y(flip=flip, u=u):
                if u == 1:
                    sent[FYM, flip] = send(near_at(1, 1, flip), near_at(1, 1, flip), ym)
                share(1, flip, u, near_at(u, 1, flip))

            add((KYP, int(flip), u), (TO_YP, flip, u), near_at(u, 3, flip), plus_y, before)
            add((KYM, int(flip), u), (TO_YM, flip, u), near_at(u, 1, flip), minus_y, before)
            key, origin = (FYP, KYP) if u == 0 else (FYM, KYM)
            add(
                (KYO, int(flip), u),
                (key, flip),
                near_at(u, 2, flip),
                lambda flip=flip, u=u: share(2, flip, u, near_at(u, 2, flip)),
                ((origin, int(flip), u),),
            )

    def near_waits():
        return [
            (sent[TO_CORE, dy, flip, u], near_at(u, dy, flip, True))
            for flip in (False, True)
            for dy in (0, 1, 3, 2)
            for u in range(2)
        ]

    def far_waits():
        waits = []
        for dz in (0, 3, 1, 2):
            waits.append((sent[TO_XM, dz, 0], far_at(0, dx=1, dz=dz)))
            waits.append((sent[TO_XP, dz, 1], far_at(1, dx=3, dz=dz)))
            waits.append((sent[FXP, dz], far_at(0, dx=2, dz=dz)))
            waits.append((sent[FXM, dz], far_at(1, dx=2, dz=dz)))
        return waits

    y_names = tuple(n for n in steps if n[0] in (KZL, KYP, KYM, KYO))
    x_names = tuple(n for n in steps if n[0] in (KZP, KZM, KZO, KXA, KXB))
    steps[(KNEAR,)] = Step(((KOWN,),) + y_names, near_waits, lambda: None)
    steps[(KFAR,)] = Step(((KOWN,),) + x_names, far_waits, lambda: None)


class RingSum:
    def __init__(self, wires, term, box, pair, plus, minus):
        self.wires, self.term, self.box, self.pair = wires, term, box, pair
        self.plus, self.minus = plus, minus

    def opposite_plus(self):
        self.opp_plus = self.wires.send(self.term(2, 0), self.box(0), self.plus)

    def opposite_minus(self):
        self.opp_minus = self.wires.send(self.term(2, 1), self.box(1), self.minus)

    def plain_plus(self):
        self.plus_sent = self.wires.send(self.term(1, 1), self.box(2), self.plus)

    def plain_minus(self):
        self.minus_sent = self.wires.send(self.term(3, 0), self.box(3), self.minus)

    def low_waits(self):
        return [(self.opp_plus, self.box(0))]

    def join_low(self):
        self.pair(0)[...] = self.term(1, 0)[...] + self.box(0)[...]
        self.low_sent = self.wires.send(self.pair(0), self.box(4), self.plus)

    def high_waits(self):
        return [(self.opp_minus, self.box(1))]

    def join_high(self):
        self.pair(1)[...] = self.term(3, 1)[...] + self.box(1)[...]
        self.high_sent = self.wires.send(self.pair(1), self.box(5), self.minus)

    def low_total_waits(self):
        return [(self.minus_sent, self.box(3)), (self.low_sent, self.box(4))]

    def high_total_waits(self):
        return [(self.plus_sent, self.box(2)), (self.high_sent, self.box(5))]

    def low_total(self):
        return self.term(0, 0)[...] + (self.box(4)[...] + self.box(3)[...])

    def high_total(self):
        return self.term(0, 1)[...] + (self.box(2)[...] + self.box(5)[...])


class SmallSum:
    def __init__(self, place, wires, slots):
        self.place, self.wires, self.slots = place, wires, slots

    def pair_out(self, stage, value, mine, peer):
        self.mine = mine
        self.slots[stage, mine] = value
        self.numbers = [self.wires.send(self.slots.at[stage, mine], self.slots.at[stage, mine], peer)]

    def pair_waits(self, stage):
        return [(self.numbers[0], self.slots.at[stage, 1 - self.mine])]

    def pair_in(self, stage):
        return self.slots[stage, 0] + self.slots[stage, 1]

    def ring_out(self, stage, value, mine, peers):
        self.mine = mine
        self.slots[stage, mine] = value
        self.numbers = [
            self.wires.send(self.slots.at[stage, mine], self.slots.at[stage, mine], peers[by])
            for by in (1, 2, 3)
        ]

    def ring_waits(self, stage):
        return [
            (number, self.slots.at[stage, lax.rem(self.mine + RING - by, RING)])
            for number, by in zip(self.numbers, (1, 2, 3))
        ]

    def ring_in(self, stage):
        return (self.slots[stage, 0] + self.slots[stage, 1]) + (self.slots[stage, 2] + self.slots[stage, 3])

    def add_steps(self, steps, kind, order, make_value, before):
        place = self.place
        places = (place.core, place.zl, place.y, place.x, place.zh)

        def out(stage, value):
            axis = order[stage]
            if axis == 0:
                self.pair_out(stage, value, places[axis], place.peer(flip_core=True))
            elif axis == 1:
                self.pair_out(stage, value, places[axis], place.peer(flip_zl=True))
            elif axis == 2:
                self.ring_out(stage, value, places[axis], {by: place.peer(dy=by) for by in (1, 2, 3)})
            elif axis == 3:
                self.ring_out(stage, value, places[axis], {by: place.peer(dx=by) for by in (1, 2, 3)})
            else:
                self.ring_out(stage, value, places[axis], {by: place.peer(dz=by) for by in (1, 2, 3)})

        def waits(stage):
            return self.pair_waits(stage) if order[stage] < 2 else self.ring_waits(stage)

        def take(stage):
            return self.pair_in(stage) if order[stage] < 2 else self.ring_in(stage)

        def last():
            self.result = take(4)

        steps[(kind, 0)] = Step(before, nothing, lambda: out(0, make_value()))
        for stage in range(1, 5):
            steps[(kind, stage)] = Step(
                ((kind, stage - 1),),
                functools.partial(waits, stage - 1),
                lambda stage=stage: out(stage, take(stage - 1)),
            )
        steps[(kind, 5)] = Step(((kind, 4),), functools.partial(waits, 4), last)


class Reduction:
    depths = (2, 1, 3, 0)

    def __init__(self, place, wires, part_rows, part_cols, boxes):
        self.place, self.wires = place, wires
        self.part_rows = part_rows
        (
            self.core_box,
            self.near_sum,
            y_box,
            y_pair,
            self.y_held,
            self.zl_box,
            x_box,
            x_pair,
            self.x_held,
            z_box,
            z_pair,
        ) = boxes
        xp, xm = place.peer(dx=1), place.peer(dx=3)
        zp, zm = place.peer(dz=1), place.peer(dz=3)
        yp, ym = place.peer(dy=1), place.peer(dy=3)
        self.zl_peer = place.peer(flip_zl=True)
        self.core_peer = place.peer(flip_core=True)

        def x_ring(k, dz):
            return RingSum(
                wires,
                lambda d, u: part_cols.at[place.row_at(d, dz) * 2 + u],
                lambda i: x_box.at[k, i],
                lambda i: x_pair.at[k, i],
                xp,
                xm,
            )

        def y_ring(flip):
            return RingSum(
                wires,
                lambda d, u: self.near_sum.at[d, int(flip), u],
                lambda i: y_box.at[int(flip), i],
                lambda i: y_pair.at[int(flip), i],
                yp,
                ym,
            )

        self.x = [x_ring(k, dz) for k, dz in enumerate(self.depths)]
        self.y = {flip: y_ring(flip) for flip in (True, False)}
        self.z = RingSum(
            wires,
            lambda d, u: self.x_held.at[self.depths.index(d), u],
            lambda i: z_box.at[i],
            lambda i: z_pair.at[i],
            zp,
            zm,
        )

    def cross_out(self):
        self.crossed = {}
        for dy in (2, 1, 3, 0):
            for flip in (True, False):
                source = self.place.col_at(dy, flip, True) * 2
                self.crossed[dy, flip] = self.wires.send(
                    self.part_rows.at[pl.ds(source, 2)],
                    self.core_box.at[dy, int(flip)],
                    self.core_peer,
                )

    def cross_waits(self, dy, flip):
        return [(self.crossed[dy, flip], self.core_box.at[dy, int(flip)])]

    def cross_in(self, dy, flip):
        source = self.place.col_at(dy, flip) * 2
        self.near_sum[dy, int(flip)] = self.part_rows[pl.ds(source, 2)] + self.core_box[dy, int(flip)]

    def low_x(self, k):
        self.x_held[k, 0] = self.x[k].low_total()

    def high_x(self, k):
        self.x_held[k, 1] = self.x[k].high_total()

    def low_y(self, flip):
        self.y_held[int(flip), 0] = self.y[flip].low_total()
        self.zl_share(flip, 0)

    def high_y(self, flip):
        self.y_held[int(flip), 1] = self.y[flip].high_total()
        self.zl_share(flip, 1)

    def zl_share(self, flip, u):
        if flip:
            self.zl_sent[u] = self.wires.send(self.y_held.at[1, u], self.zl_box.at[u], self.zl_peer)

    def finish(self, u):
        total = self.z.high_total() if u else self.z.low_total()
        self.result[u] = total + (self.y_held[0, u] + self.zl_box[u])

    def add_steps(self, steps):
        self.zl_sent, self.result = {}, {}
        for k, ring in enumerate(self.x):
            steps[(KOP, k)] = Step(((KCOLS,),), nothing, ring.opposite_plus)
            steps[(KOM, k)] = Step(((KCOLS,),), nothing, ring.opposite_minus)
            steps[(KPP, k)] = Step(((KCOLS,),), nothing, ring.plain_plus)
            steps[(KPM, k)] = Step(((KCOLS,),), nothing, ring.plain_minus)
            steps[(KRL, k)] = Step(((KOP, k),), ring.low_waits, ring.join_low)
            steps[(KRH, k)] = Step(((KOM, k),), ring.high_waits, ring.join_high)
            steps[(KTA, k)] = Step(
                ((KRL, k), (KPM, k)), ring.low_total_waits, functools.partial(self.low_x, k)
            )
            steps[(KTB, k)] = Step(
                ((KRH, k), (KPP, k)), ring.high_total_waits, functools.partial(self.high_x, k)
            )
        steps[(KCO,)] = Step(((KROWS,),), nothing, self.cross_out)
        for flip in (True, False):
            f = int(flip)
            ring = self.y[flip]
            for dy in (2, 1, 3, 0):
                steps[(KCI, dy, f)] = Step(
                    ((KCO,),),
                    functools.partial(self.cross_waits, dy, flip),
                    functools.partial(self.cross_in, dy, flip),
                )
            steps[(KQO, f)] = Step(((KCI, 2, f),), nothing, ring.opposite_plus)
            steps[(KQM, f)] = Step(((KCI, 2, f),), nothing, ring.opposite_minus)
            steps[(KQP, f)] = Step(((KCI, 1, f),), nothing, ring.plain_plus)
            steps[(KQN, f)] = Step(((KCI, 3, f),), nothing, ring.plain_minus)
            steps[(KQL, f)] = Step(((KQO, f), (KCI, 1, f)), ring.low_waits, ring.join_low)
            steps[(KQH, f)] = Step(((KQM, f), (KCI, 3, f)), ring.high_waits, ring.join_high)
            steps[(KQA, f)] = Step(
                ((KQL, f), (KQN, f), (KCI, 0, f)),
                ring.low_total_waits,
                functools.partial(self.low_y, flip),
            )
            steps[(KQB, f)] = Step(
                ((KQH, f), (KQP, f), (KCI, 0, f)),
                ring.high_total_waits,
                functools.partial(self.high_y, flip),
            )
        steps[(KWO,)] = Step(((KTA, 0),), nothing, self.z.opposite_plus)
        steps[(KWQ,)] = Step(((KTB, 0),), nothing, self.z.opposite_minus)
        steps[(KWP,)] = Step(((KTB, 1),), nothing, self.z.plain_plus)
        steps[(KWM,)] = Step(((KTA, 2),), nothing, self.z.plain_minus)
        steps[(KWL,)] = Step(((KWO,), (KTA, 1)), self.z.low_waits, self.z.join_low)
        steps[(KWH,)] = Step(((KWQ,), (KTB, 2)), self.z.high_waits, self.z.join_high)
        steps[(KE, 0)] = Step(
            ((KWM,), (KWL,), (KTA, 3), (KQA, 0), (KQA, 1)),
            lambda: [(self.zl_sent[0], self.zl_box.at[0])] + self.z.low_total_waits(),
            lambda: self.finish(0),
        )
        steps[(KE, 1)] = Step(
            ((KWP,), (KWH,), (KTB, 3), (KQB, 0), (KQB, 1)),
            lambda: [(self.zl_sent[1], self.zl_box.at[1])] + self.z.high_total_waits(),
            lambda: self.finish(1),
        )


def reduce_scratch(K, T):
    return [
        pltpu.VMEM((4, 2, 2, K, T), F32),
        pltpu.VMEM((4, 2, 2, K, T), F32),
        pltpu.VMEM((2, 6, K, T), F32),
        pltpu.VMEM((2, 2, K, T), F32),
        pltpu.VMEM((2, 2, K, T), F32),
        pltpu.VMEM((2, K, T), F32),
        pltpu.VMEM((4, 6, K, T), F32),
        pltpu.VMEM((4, 2, K, T), F32),
        pltpu.VMEM((4, 2, K, T), F32),
        pltpu.VMEM((6, K, T), F32),
        pltpu.VMEM((2, K, T), F32),
    ]


def split(value):
    high = value.astype(BF16)
    low = (value - high.astype(F32)).astype(BF16)
    return high, low


def dot_t(left, right, precision=None):
    return lax.dot_general(
        left, right, (((1,), (1,)), ((), ())), precision=precision, preferred_element_type=F32
    )


def dot_n(left, right, precision=None):
    return lax.dot_general(
        left, right, (((1,), (0,)), ((), ())), precision=precision, preferred_element_type=F32
    )


def fold(square):
    half = square.shape[0] // 2
    return jnp.concatenate([square[:half], square[half:]], axis=1)


def unfold(flat):
    half = flat.shape[1] // 2
    return jnp.concatenate([flat[:, :half], flat[:, half:]], axis=0)


def energy(part, vectors):
    K = part.shape[1]
    group = 4

    def step(g, total):
        left = [jnp.concatenate(split(part[g * group + i]), axis=0) for i in range(group)]
        right = [jnp.concatenate(split(vectors[g * group + i]), axis=0) for i in range(group)]
        return total + dot_t(jnp.concatenate(left, axis=1), jnp.concatenate(right, axis=1))

    total = lax.fori_loop(0, part.shape[0] // group, step, jnp.zeros((2 * K, 2 * K), F32))
    total = total[:K] + total[K:]
    total = total[:, :K] + total[:, K:]
    return total + total.T


class Application:
    def __init__(
        self, place, wires, table, pairs, sums, near, far, part_rows, part_cols, boxes, slots, early_slots
    ):
        self.place, self.wires, self.table, self.pairs, self.sums = place, wires, table, pairs, sums
        self.near, self.far = near, far
        self.part_rows, self.part_cols = part_rows, part_cols
        self.slots, self.early_slots = slots, early_slots
        self.reduction = Reduction(place, wires, part_rows, part_cols, boxes)

    def products(self, vectors, ids, before, transposed, start, stop):
        K = self.near.shape[1]
        dot = dot_t if transposed else dot_n

        def product(s):
            high, low = split(vectors[self.table[ids, s]])
            both = dot(jnp.concatenate([high, low], axis=0), self.pairs[s, 0])
            return (both[:K] + both[K:]) + dot(high, self.pairs[s, 1])

        def step(group, carry):
            slots = [group * UNROLL + i for i in range(UNROLL)]
            for s, value in zip(slots, [product(s) for s in slots]):
                self.sums[s + 1] = value + self.sums[self.table[before, s]]
            return carry

        lax.fori_loop(start // UNROLL, stop // UNROLL, step, 0)

    def upper(self, start, stop):
        self.products(self.near, 0, 3, False, start, stop)

    def lower(self, start, stop):
        self.products(self.far, 1, 2, True, start, stop)

    def collect(self, line, parts):
        def step(group, carry):
            for i in range(4):
                p = group * 4 + i
                parts[p] = self.sums[self.table[line, p]]
            return carry

        lax.fori_loop(0, parts.shape[0] // 4, step, 0)

    def steps(self, own, place_own, prepare, early):
        steps = {}
        gather_steps(self.place, self.wires, own, self.near, self.far, steps)
        steps[(KOWN,)] = Step(((KSTART,),), nothing, place_own)
        ready = ()
        for i, chunk in enumerate(prepare):
            steps[(KP, i)] = Step(ready, nothing, chunk)
            ready = ((KP, i),)
        last = ((KNEAR,),) + ready
        for i in range(CHUNKS):
            size = self.pairs.shape[0] // CHUNKS
            act = functools.partial(self.upper, i * size, (i + 1) * size)
            steps[(KU, i)] = Step(last, nothing, act)
            last = ((KU, i),)
        steps[(KCOLS,)] = Step(last, nothing, lambda: self.collect(5, self.part_cols))
        last = ((KFAR,), (KCOLS,))
        for i in range(CHUNKS):
            act = functools.partial(self.lower, i * size, (i + 1) * size)
            steps[(KL, i)] = Step(last, nothing, act)
            last = ((KL, i),)
        steps[(KROWS,)] = Step(last, nothing, lambda: self.collect(4, self.part_rows))
        self.reduction.add_steps(steps)
        self.small = SmallSum(self.place, self.wires, self.slots)
        self.early = SmallSum(self.place, self.wires, self.early_slots)
        self.small.add_steps(
            steps,
            KS,
            SUM_ORDER,
            lambda: fold(energy(self.part_cols, self.far)),
            ((KFAR,), (KCOLS,)),
        )
        if early is not None:
            self.early.add_steps(steps, KT, EARLY_ORDER, early, ((KOWN,),))
        return steps

    def run(self, order, own, place_own, prepare, early):
        steps = self.steps(own, place_own, prepare, early)
        names = list(steps)
        done = set()
        for number in order:
            name = names[number]
            assert set(steps[name].before) <= done and name not in done, name
            steps[name].run(self.wires)
            done.add(name)
        assert len(done) == len(steps)
        return self.reduction.result, self.small.result


def whole_kernel(
    total_rows, live, row_ids, col_ids, row_line, col_line, tiles, block, image_x, image_w, grams, *scratch
):
    lines, table, table_sem, *scratch = scratch
    (stage, stage_sems, pairs, sums, resid, early_slots, send_sems, recv_sems), scratch = (
        scratch[:8],
        scratch[8:],
    )
    sets = scratch[: len(scratch) // 2], scratch[len(scratch) // 2 :]
    place = Place()
    K, width = block.shape
    T = width // 2
    count = tiles.shape[0]
    depth = stage.shape[0]

    def fetch(s, slot):
        return pltpu.make_async_copy(tiles.at[s], stage.at[slot], stage_sems.at[slot])

    for s in range(depth):
        fetch(s, s).start()
    fill_lines(live[0], row_ids, col_ids, row_line, col_line, lines)
    to_scalars = pltpu.make_async_copy(lines, table, table_sem)
    to_scalars.start()
    greet(near_peers(place) + sum_peers(place))
    to_scalars.wait()
    wires = Wires(place, send_sems, recv_sems)

    def split_tiles(start, stop, more):
        def step(s, carry):
            slot = lax.rem(s, depth)
            fetch(s, slot).wait()
            pairs[s, 0], pairs[s, 1] = split(stage[slot])
            if more:
                fetch(s + depth, slot).start()
            return carry

        lax.fori_loop(start, stop, step, 0)

    prepare = [
        functools.partial(split_tiles, start, start + PREPARE, start + PREPARE + depth <= count)
        for start in range(0, count, PREPARE)
    ]

    def apply(number):
        near, far, part_rows, part_cols, slots, *boxes = sets[number]
        return Application(
            place, wires, table, pairs, sums, near, far, part_rows, part_cols, boxes, slots, early_slots
        )

    sums[0] = jnp.zeros((K, T), F32)
    first = apply(0)

    def place_block():
        for u in range(2):
            half = block[:, u * T : (u + 1) * T]
            first.near[place.col * 2 + u] = half
            first.far[place.row * 2 + u] = half

    halves, total = first.run(
        FIRST_ORDER,
        lambda u: block.at[:, pl.ds(u * T, T)], place_block, prepare, None
    )
    mean = unfold(total) / total_rows
    for u in range(2):
        resid[u] = halves[u] - dot_n(mean, block[:, u * T : (u + 1) * T], HIGHEST)
    second = apply(1)
    local = {}

    def place_resid():
        grams[0] = mean
        cross = jnp.zeros((K, K), F32)
        square = jnp.zeros((K, K), F32)
        for u in range(2):
            image_x[:, u * T : (u + 1) * T] = halves[u]
            value = resid[u]
            second.near[place.col * 2 + u] = value
            second.far[place.row * 2 + u] = value
            cross += dot_t(halves[u], value, HIGHEST)
            square += dot_t(value, value, HIGHEST)
        grams[1] = cross
        grams[3] = square

    def early():
        return jnp.concatenate([fold(grams[1]), fold(grams[3])], axis=0)

    halves, total = second.run(
        SECOND_ORDER, lambda u: resid.at[u], place_resid, (), early
    )
    for u in range(2):
        image_w[:, u * T : (u + 1) * T] = halves[u]
    half = K // 2
    grams[1] = unfold(second.early.result[:half]) / total_rows
    grams[2] = unfold(total) / total_rows
    grams[3] = unfold(second.early.result[half:]) / total_rows
    wires.drain()


def fill_lines(live, row_ids, col_ids, row_line, col_line, lines):
    slots = row_line.shape[1]
    lane = lax.broadcasted_iota(jnp.int32, row_line.shape, 1)
    rows, cols = row_line[...], col_line[...]
    none = jnp.zeros_like(rows)

    def step(t, carry):
        before_row, before_col, last_row, last_col = carry
        alive = t < live
        row = jnp.where(alive, row_ids[t], -1)
        col = jnp.where(alive, col_ids[t], -1)
        later = lane > t
        number = t + 1
        return (
            jnp.where(jnp.logical_and(rows == row, later), number, before_row),
            jnp.where(jnp.logical_and(cols == col, later), number, before_col),
            jnp.where(lane == row, number, last_row),
            jnp.where(lane == col, number, last_col),
        )

    lines[...] = jnp.zeros_like(lines)
    found = lax.fori_loop(0, slots, step, (none, none, none, none))
    for line, value in enumerate((rows, cols) + found):
        lines[line : line + 1, :slots] = value


def hand_over(*refs):
    half = len(refs) // 2
    for source, target in zip(refs[:half], refs[half:]):
        target[...] = source[...]


def vmem(count):
    return [pl.BlockSpec(memory_space=pltpu.VMEM)] * count


def on_device(tile_count, tile_rows, tile_cols, tiles, block):
    K, width = block.shape
    T = tiles.shape[-1]
    slots = tiles.shape[2]
    total_rows = width * lax.axis_size("row") * lax.axis_size("col")
    smem = pl.BlockSpec(memory_space=pltpu.SMEM)
    strip = pltpu.VMEM((32, K, T), F32)
    seg = jax.ShapeDtypeStruct((K, width), F32)

    one_set = [strip] * 4 + [pltpu.VMEM((5, 4, K // 2, 2 * K), F32)] + reduce_scratch(K, T)

    shapes = (seg, seg, jax.ShapeDtypeStruct((4, K, K), F32))
    results = pl.pallas_call(
        functools.partial(whole_kernel, total_rows),
        out_shape=shapes,
        in_specs=[smem] * 3 + vmem(2) + [pl.BlockSpec(memory_space=pl.ANY)] + vmem(1),
        out_specs=tuple(vmem(3)),
        scratch_shapes=[
            pltpu.VMEM((8, 128), jnp.int32),
            pltpu.SMEM((8, 128), jnp.int32),
            pltpu.SemaphoreType.DMA,
            pltpu.VMEM((STAGE, T, T), F32),
            pltpu.SemaphoreType.DMA((STAGE,)),
            pltpu.VMEM((slots, 2, T, T), BF16),
            pltpu.VMEM((slots + 1, K, T), F32),
            pltpu.VMEM((2, K, T), F32),
            pltpu.VMEM((5, 4, K, 2 * K), F32),
            pltpu.SemaphoreType.DMA((300,)),
            pltpu.SemaphoreType.DMA((300,)),
        ]
        + one_set * 2,
        compiler_params=pltpu.CompilerParams(
            collective_id=0, has_side_effects=True, vmem_limit_bytes=VMEM_LIMIT
        ),
        name="rayleigh_ritz",
    )(
        tile_count[0],
        tile_rows[0, 0],
        tile_cols[0, 0],
        tile_rows[0],
        tile_cols[0],
        tiles[0, 0],
        block,
    )
    return pl.pallas_call(
        hand_over,
        out_shape=shapes,
        in_specs=vmem(3),
        out_specs=tuple(vmem(3)),
        name="hand_over",
    )(*results)


def solution(mesh):
    return jax.shard_map(
        on_device,
        mesh=mesh,
        in_specs=(
            P("row", "col"),
            P("row", "col", None),
            P("row", "col", None),
            P("row", "col", None, None, None),
            P(None, ("row", "col")),
        ),
        out_specs=(P(None, ("row", "col")), P(None, ("row", "col")), P()),
        check_vma=False,
    )
```
